32 devices in a mesh: tm: 2 (over y), pts: 16 (over z, x, core).
Axes of the slice: x: 2, y: 2, z: 4, core: 2. Of those that a mesh axis runs over, the one named last changes fastest.
Arguments:
- precip: float32 [512, 16384], P('tm', 'pts'), may hold values from -150 to 300, as said below
- thresholds: float32 [64], replicated, may hold values from -1 to 5
- bin_index: int32 [16384], P('pts'), may hold values from 0 to 63
- test_matrix: float32 [512, 256], P('tm'), may hold values from -0.25 to 0.25
Outputs:
- basis: float32 [16384, 256], P(('pts', 'tm'))
- factor: float32 [256, 256], replicated
The draws below stay inside these ranges and needn't reach their ends.
Inputs may be any that keep to these rules, and one draw needn't show every extreme that they name: `precip`: precipitation records.
All inputs are finite; a program needn't handle non-finite values.
Results may differ from the reference program's by a relative error of at most 0.0003.
Values sent between devices are 32-bit elements; how exact they have to be, the bound alone decides.
No kernel may reach another device: no remote copies, remote signals or barrier semaphores. Data moves between devices by JAX's collectives and lax.ppermute only.
A program may use at most 64 MiB of HBM per device.

```python
import math
import jax
import jax.numpy as jnp
from jax import lax

K = 256
HARM = 8
NBINS = 64
DAYS = 512
POINTS = 16384


def draw_precip(key, part):
    keys = jax.random.split(key, 5)
    position = jnp.arange(POINTS, dtype=jnp.float32) / max(POINTS - 1, 1)
    spread = jnp.exp(jax.random.uniform(keys[0], (POINTS,), minval=0.0, maxval=math.log(10.0)))
    scaling = spread * jnp.exp(math.log(3.0) * position)
    amplitude = jax.random.uniform(keys[1], (POINTS,), minval=0.5, maxval=2.0)
    shifted = jax.random.uniform(keys[2], (POINTS,), minval=-math.pi, maxval=math.pi)
    day_number = jnp.arange(DAYS, dtype=jnp.float32)[:, None]
    season = amplitude[None, :] * jnp.cos(2.0 * math.pi / 365.25 * day_number + shifted[None, :])
    baseline = jax.random.uniform(keys[3], (POINTS,), minval=1.0, maxval=3.0)
    noise = jnp.clip(jax.random.normal(keys[4], (DAYS, POINTS), jnp.float32), -4.0, 4.0)
    values = scaling[None, :] * (baseline[None, :] + season + noise)
    return values.astype(jnp.float32)


def with_ends(result, rng, least, high):
    longest = result.shape.index(max(result.shape))
    spots = []
    for shift in (0, 1):
        where = [jax.random.randint(jax.random.fold_in(rng, axis), (), 0, length) for axis, length in enumerate(result.shape)]
        where[longest] = (where[longest] + shift) % result.shape[longest]
        spots.append(tuple(where))
    return result.at[spots[0]].set(least).at[spots[1]].set(high)


def block_scale(rng, extent, pieces, least, high):
    gain = 1.0
    for dim, parts in pieces:
        heights = jax.random.uniform(jax.random.fold_in(jax.random.fold_in(rng, 6), dim), (parts,), jnp.float32, least / len(pieces), high / len(pieces))
        gain = gain * jnp.repeat(jnp.exp(heights), extent[dim] // parts).reshape((-1,) + (1,) * (len(extent) - 1 - dim))
    return gain


def gaussian(own_key, shape, width, bound, cuts=(), kind=jnp.bfloat16):
    array = width * jax.random.normal(own_key, shape, jnp.float32)
    if cuts:
        array = array * block_scale(own_key, shape, cuts, -0.22, 0.18)
    return jnp.clip(array, -bound, bound).astype(kind)


def setup_inputs(seed: int = 0) -> dict:
    key_of = jax.random.split(jax.random.key(seed), 5)
    return {
        "precip": draw_precip(jax.random.fold_in(key_of[4], 71), 0),
        "thresholds": jnp.clip(jax.random.uniform(key_of[1], (NBINS,), jnp.float32, -1.0, 5.0), -1.0, 5.0),
        "bin_index": with_ends(jax.random.randint(key_of[2], (POINTS,), 0, NBINS), jax.random.fold_in(key_of[2], 1), 0, NBINS - 1).astype(jnp.int32),
        "test_matrix": gaussian(key_of[3], (DAYS, K), DAYS ** -0.5, 0.25, ((0, 2),), jnp.float32),
    }


year_days = 365.25

def harmonic_table(day_number):
    phase_base = day_number.astype(jnp.float32)
    columns = [jnp.ones_like(phase_base)]
    for order in range(1, HARM + 1):
        phase = 2.0 * math.pi * order / year_days * phase_base
        columns.append(jnp.cos(phase))
        columns.append(jnp.sin(phase))
    return jnp.stack(columns, 0)

def normal_solve(factor_low, values):
    forward = lax.linalg.triangular_solve(factor_low, values, left_side=True, lower=True)
    return lax.linalg.triangular_solve(factor_low, forward, left_side=True, lower=True, transpose_a=True)

def reference(precip, thresholds, bin_index, test_matrix):
    highest = lax.Precision.HIGHEST
    harmonic_cols = harmonic_table(jnp.arange(DAYS, dtype=jnp.int32))
    normal = jnp.dot(harmonic_cols, harmonic_cols.T, precision=highest)
    projections = jnp.dot(harmonic_cols, precip, precision=highest)
    coefficients = normal_solve(jnp.linalg.cholesky(normal), projections)
    anomaly = precip - jnp.dot(harmonic_cols.T, coefficients, precision=highest)
    level = thresholds[bin_index]
    excess = jnp.maximum(anomaly - level[None, :], 0.0)
    sketch = lax.dot_general(excess, test_matrix, (((0,), (0,)), ((), ())), precision=highest)
    cross = jnp.dot(sketch.T, sketch, precision=highest) / POINTS
    lower = jnp.linalg.cholesky(cross)
    basis = lax.linalg.triangular_solve(lower, sketch, left_side=False, lower=True, transpose_a=True)
    return (basis, lower.T)
```

```python
import math

import jax
import jax.numpy as jnp
from jax import lax
from jax.sharding import PartitionSpec as P

HARM = 8


year_days = 365.25


def harmonic_table(day_number):
    phase_base = day_number.astype(jnp.float32)
    columns = [jnp.ones_like(phase_base)]
    for order in range(1, HARM + 1):
        phase = 2.0 * math.pi * order / year_days * phase_base
        columns.append(jnp.cos(phase))
        columns.append(jnp.sin(phase))
    return jnp.stack(columns, 0)


def normal_solve(factor_low, values):
    forward = lax.linalg.triangular_solve(factor_low, values, left_side=True, lower=True)
    return lax.linalg.triangular_solve(
        factor_low, forward, left_side=True, lower=True, transpose_a=True
    )


AXES = ("tm", "pts")


def swap(value, bit):
    total = lax.axis_size("tm") * lax.axis_size("pts")
    return lax.ppermute(value, AXES, [(i, i ^ bit) for i in range(total)])


def all_days(block, count, place, stride):
    pieces = [block] + [swap(block, step * stride) for step in range(1, count)]
    stack = jnp.stack(pieces)
    order = place ^ jnp.arange(count)
    return stack[order].reshape((-1,) + block.shape[1:])


def sum_all(value):
    total = lax.axis_size("tm") * lax.axis_size("pts")
    low = lax.axis_index("pts") % 2
    half = value.shape[0] // 2
    kept = lax.dynamic_slice_in_dim(value, low * half, half, 0)
    sent = lax.dynamic_slice_in_dim(value, (1 - low) * half, half, 0)
    part = kept + swap(sent, 1)
    bit = 2
    while bit < total:
        part = part + swap(part, bit)
        bit *= 2
    other = swap(part, 1)
    return jnp.where(
        low == 0,
        jnp.concatenate([part, other], 0),
        jnp.concatenate([other, part], 0),
    )


def on_device(precip, thresholds, bin_index, test_matrix):
    highest = lax.Precision.HIGHEST
    tm_count = lax.axis_size("tm")
    tm_place = lax.axis_index("tm")
    days_local, points_local = precip.shape
    own_rows = points_local // tm_count
    days_total = days_local * tm_count
    points_total = points_local * lax.axis_size("pts")
    full_table = harmonic_table(jnp.arange(days_total, dtype=jnp.int32))
    normal = jnp.dot(full_table, full_table.T, precision=highest)
    normal_low = jnp.linalg.cholesky(normal)
    one_hot = (
        bin_index[:, None] == jnp.arange(thresholds.shape[0], dtype=jnp.int32)[None, :]
    ).astype(jnp.float32)
    level_local = jnp.dot(one_hot, thresholds, precision=highest)
    series = lax.all_to_all(precip, "tm", split_axis=1, concat_axis=0, tiled=True)
    projections = jnp.dot(full_table, series, precision=highest)
    coefficients = normal_solve(normal_low, projections)
    anomaly = series - lax.dot_general(
        full_table, coefficients, (((0,), (0,)), ((), ())), precision=highest
    )
    level_own = lax.dynamic_slice_in_dim(level_local, tm_place * own_rows, own_rows, 0)
    excess = jnp.maximum(anomaly - level_own[None, :], 0.0)
    sketch = lax.dot_general(
        excess,
        all_days(test_matrix, tm_count, tm_place, lax.axis_size("pts")),
        (((0,), (0,)), ((), ())),
        precision=highest,
    )
    local_cross = jnp.dot(sketch.T, sketch, precision=highest)
    cross = sum_all(local_cross) / points_total
    lower = jnp.linalg.cholesky(cross)
    basis = lax.linalg.triangular_solve(
        lower, sketch, left_side=False, lower=True, transpose_a=True
    )
    return (basis, lower.T)


def solution(mesh):
    in_specs = (P("tm", "pts"), P(), P("pts"), P("tm", None))
    out_specs = (P(("pts", "tm"), None), P())
    return jax.shard_map(
        on_device, mesh=mesh, in_specs=in_specs, out_specs=out_specs, check_vma=False
    )
```

```python
import functools
import math

import jax
import jax.numpy as jnp
import numpy as np
from jax import lax
from jax.experimental import pallas as pl
from jax.experimental.pallas import tpu as pltpu
from jax.sharding import PartitionSpec as P

HARM = 8
SUB = 8
AXES = ("tm", "pts")
HI = lax.Precision.HIGHEST

year_days = 365.25


def harmonic_filter(days_total):
    phase_base = np.arange(days_total).astype(np.float32)
    columns = [np.ones_like(phase_base)]
    for order in range(1, HARM + 1):
        phase = np.float32(2.0 * math.pi * order / year_days) * phase_base
        columns.append(np.cos(phase.astype(np.float64)))
        columns.append(np.sin(phase.astype(np.float64)))
    table = np.stack(columns, 0).astype(np.float32).astype(np.float64)
    low = np.linalg.cholesky(table @ table.T)
    rows = np.linalg.solve(low, table)
    padded = -(-rows.shape[0] // SUB) * SUB
    rows = np.concatenate([rows, np.zeros((padded - rows.shape[0], days_total))], 0)
    return rows.astype(np.float32)


def nn(a, b):
    return jnp.dot(a, b, precision=HI, preferred_element_type=jnp.float32)


def nt(a, b):
    return lax.dot_general(
        a, b, (((1,), (1,)), ((), ())), precision=HI, preferred_element_type=jnp.float32
    )


def tn(a, b):
    return lax.dot_general(
        a, b, (((0,), (0,)), ((), ())), precision=HI, preferred_element_type=jnp.float32
    )


def swap(value, bit):
    total = lax.axis_size("tm") * lax.axis_size("pts")
    return lax.ppermute(value, AXES, [(i, i ^ bit) for i in range(total)])


def front_kernel(start, own_rows, tm_count, first, last, *refs):
    refs = list(refs)
    take = lambda n: [refs.pop(0) for _ in range(n)]
    (days_ref, thr_ref, bin_ref, filt_ref, filt_t_ref, test_ref) = take(6)
    recv_refs = take(tm_count - 1)
    half_refs = take(2 * (tm_count - 1))
    acc_ref = None if first else take(1)[0]
    sketch_ref = take(1)[0]
    outs = take(2) if last else take(1)
    own_ref, table_ref, sem = take(3)
    width = own_ref.shape[1]
    days_local = own_ref.shape[0]
    place = lax.axis_index("tm")
    low = lax.axis_index("pts") % 2
    at = pl.multiple_of(place * own_rows + start, math.gcd(own_rows, start) if start else own_rows)
    copy = pltpu.make_async_copy(days_ref.at[:, pl.ds(at, width)], own_ref, sem)
    copy.start()
    table_ref[:days_local, :] = test_ref[...]
    half = days_local // 2
    for k in range(tm_count - 1):
        base = days_local * (k + 1)
        table_ref[pl.ds(pl.multiple_of(base + low * half, half), half), :] = half_refs[2 * k][...]
        table_ref[pl.ds(pl.multiple_of(base + (1 - low) * half, half), half), :] = half_refs[2 * k + 1][...]
    bins = bin_ref[:, pl.ds(at, width)]
    count = thr_ref.shape[0]
    entry = lax.broadcasted_iota(jnp.int32, (count, width), 0)
    level = jnp.sum(jnp.where(entry == bins, thr_ref[...], 0.0), axis=0, keepdims=True)
    copy.wait()
    series = [own_ref[...]] + [r[...] for r in recv_refs]
    proj = nn(filt_ref[place], series[0])
    for k in range(1, tm_count):
        proj = proj + nn(filt_ref[place ^ k], series[k])
    excess = [
        jnp.maximum(series[k] - nn(filt_t_ref[place ^ k], proj) - level, 0.0)
        for k in range(tm_count)
    ]
    sketch = tn(jnp.concatenate(excess, 0), table_ref[...])
    sketch_ref[...] = sketch
    cross = tn(sketch, sketch)
    if not first:
        cross = cross + acc_ref[...]
    if not last:
        outs[0][...] = cross
        return
    kept_ref, sent_ref = outs
    tile = cross.shape[0] // 2
    row = lax.broadcasted_iota(jnp.int32, (tile, tile), 0)
    col = lax.broadcasted_iota(jnp.int32, (tile, tile), 1)
    second = cross[tile:, tile:]
    ends = jnp.where(row >= col, cross[:tile, :tile], second)
    side = cross[tile:, :tile]
    diag = jnp.broadcast_to(
        jnp.sum(jnp.where(row == col, second, 0.0), axis=0, keepdims=True), (SUB, tile)
    )
    kept_ref[:tile, :] = jnp.where(low == 0, ends, side)
    sent_ref[:tile, :] = jnp.where(low == 0, side, ends)
    kept_ref[tile:, :] = diag
    sent_ref[tile:, :] = diag


def over_lanes(value, col, tile):
    return jnp.broadcast_to(value[:, col:col + 1], (SUB, tile))


def over_rows(value, row, tile):
    return jnp.broadcast_to(value[row:row + 1, :], (SUB, tile))


def panel(blocks):
    count = len(blocks)
    blocks = list(blocks)
    tile = count * SUB
    lane = lax.broadcasted_iota(jnp.int32, (SUB, tile), 1)
    row = lax.broadcasted_iota(jnp.int32, (SUB, tile), 0)
    upper, inverse = [], []
    for i in range(count):
        first = SUB * i
        own = blocks[i]
        cols = [over_lanes(own, first + k, tile) for k in range(SUB)]
        e = {(j, k): over_rows(cols[k], j, tile) for k in range(SUB) for j in range(k + 1)}
        inside = (lane >= first) & (lane < first + SUB)
        later = {
            t: [over_lanes(blocks[t], first + k, tile) for k in range(SUB)]
            for t in range(i + 1, count)
        }
        rows = [
            jnp.where(inside, jnp.where(lane == first + j, 1.0, 0.0), over_rows(own, j, tile))
            for j in range(SUB)
        ]
        for j in range(SUB):
            s = lax.rsqrt(e[j, j])
            fac = {k: e[j, k] * s for k in range(j + 1, SUB)}
            e[j, j] = e[j, j] * s
            rows[j] = rows[j] * s
            for t in later:
                later[t][j] = later[t][j] * s
            for k in range(j + 1, SUB):
                e[j, k] = fac[k]
                for m in range(k, SUB):
                    e[k, m] = e[k, m] - fac[k] * fac[m]
                rows[k] = rows[k] - fac[k] * rows[j]
                for t in later:
                    later[t][k] = later[t][k] - fac[k] * later[t][j]
        for t in later:
            terms = [later[t][j] * rows[j] for j in range(SUB)]
            while len(terms) > 1:
                terms = [terms[q] + terms[q + 1] for q in range(0, len(terms), 2)]
            blocks[t] = jnp.where(inside, 0.0, blocks[t]) - terms[0]
        up = jnp.zeros((SUB, tile), jnp.float32)
        inv = up
        for j in range(SUB):
            line = jnp.where(lane >= first + SUB, rows[j], 0.0)
            for k in range(j, SUB):
                line = jnp.where(lane == first + k, e[j, k], line)
            up = jnp.where(row == j, line, up)
            inv = jnp.where(row == j, rows[j], inv)
        upper.append(up)
        inverse.append(jnp.where(lane < first + SUB, inv, 0.0))
    return jnp.concatenate(upper, 0), jnp.concatenate(inverse, 0)


def back_kernel(points_total, chunks, part_ref, other_ref, *refs):
    sketch_refs = refs[:chunks]
    basis_ref, factor_ref = refs[chunks:]
    tile = part_ref.shape[1]
    low = lax.axis_index("pts") % 2
    part = part_ref[...] / points_total
    other = other_ref[...] / points_total
    ends = jnp.where(low == 0, part[:tile], other[:tile])
    side = jnp.where(low == 0, other[:tile], part[:tile])
    diag = jnp.where(low == 0, other[tile:tile + 1], part[tile:tile + 1])
    row = lax.broadcasted_iota(jnp.int32, (tile, tile), 0)
    col = lax.broadcasted_iota(jnp.int32, (tile, tile), 1)
    ends_t = ends.T
    side_t = side.T
    split = lambda a: [a[SUB * t:SUB * (t + 1), :] for t in range(tile // SUB)]
    up, inv1 = panel(split(jnp.where(row >= col, ends, ends_t)))
    factor_ref[:tile, :tile] = up
    factor_ref[tile:, :tile] = jnp.zeros((tile, tile), jnp.float32)
    right = nn(inv1, side_t)
    right_t = nt(side, inv1)
    factor_ref[:tile, tile:] = right
    rest = jnp.where(row < col, ends, jnp.where(row == col, diag, ends_t)) - nn(right_t, right)
    up, inv2 = panel(split(rest))
    factor_ref[tile:, tile:] = up
    at = 0
    for ref in sketch_refs:
        size = ref.shape[0]
        left = nt(ref[:, :tile], inv1)
        basis_ref[at:at + size, :tile] = left
        basis_ref[at:at + size, tile:] = nt(ref[:, tile:] - nn(left, right), inv2)
        at += size


def chunk_widths(own_rows):
    last = own_rows // 4
    if last % 128:
        return [own_rows]
    return [own_rows - last, last]


def on_device(precip, thresholds, bin_index, test_matrix):
    tm_count = lax.axis_size("tm")
    pts_count = lax.axis_size("pts")
    place = lax.axis_index("tm")
    low = lax.axis_index("pts") % 2
    days_local, points_local = precip.shape
    columns = test_matrix.shape[1]
    tile = columns // 2
    own_rows = points_local // tm_count
    days_total = days_local * tm_count
    points_total = points_local * pts_count
    f32 = jnp.float32

    rows = harmonic_filter(days_total)
    filt = rows.reshape(rows.shape[0], tm_count, days_local).transpose(1, 0, 2)
    filt_t = jnp.asarray(filt.transpose(0, 2, 1))
    filt = jnp.asarray(filt)
    thr = thresholds[:, None]
    bins = bin_index[None, :]

    half = days_local // 2
    mine = lax.dynamic_slice_in_dim(test_matrix, low * half, half, 0)
    halves = []
    for k in range(1, tm_count):
        halves.append(swap(mine, k * pts_count))
    halves = [h for got in halves for h in (got, swap(got, 1))]

    vmem = pl.BlockSpec(memory_space=pltpu.VMEM)
    start = 0
    widths = chunk_widths(own_rows)
    received = []
    for width in widths:
        received.append(
            [
                swap(
                    lax.dynamic_slice_in_dim(precip, (place ^ k) * own_rows + start, width, 1),
                    k * pts_count,
                )
                for k in range(1, tm_count)
            ]
        )
        start += width

    sketches = []
    cross = None
    start = 0
    for index, width in enumerate(widths):
        first, last = index == 0, index == len(widths) - 1
        operands = [precip, thr, bins, filt, filt_t, test_matrix] + received[index] + halves
        specs = [pl.BlockSpec(memory_space=pl.ANY)] + [vmem] * (len(operands) - 1)
        if not first:
            operands.append(cross)
            specs.append(vmem)
        shapes = [jax.ShapeDtypeStruct((width, columns), f32)]
        if last:
            shapes += [jax.ShapeDtypeStruct((tile + SUB, tile), f32)] * 2
        else:
            shapes += [jax.ShapeDtypeStruct((columns, columns), f32)]
        out = pl.pallas_call(
            functools.partial(front_kernel, start, own_rows, tm_count, first, last),
            out_shape=shapes,
            in_specs=specs,
            out_specs=[vmem] * len(shapes),
            scratch_shapes=[
                pltpu.VMEM((days_local, width), f32),
                pltpu.VMEM((days_total, columns), f32),
                pltpu.SemaphoreType.DMA,
            ],
            cost_estimate=pl.CostEstimate(
                flops=12 * width * columns * (days_total + columns),
                bytes_accessed=4 * days_total * (width + columns),
                transcendentals=0,
            ),
            name=f"front{index}",
        )(*operands)
        sketches.append(out[0])
        cross = out[1]
        start += width
    kept, sent = out[1], out[2]

    part = kept + swap(sent, 1)
    bit = 2
    while bit < tm_count * pts_count:
        part = part + swap(part, bit)
        bit *= 2
    other = swap(part, 1)

    basis, factor = pl.pallas_call(
        functools.partial(back_kernel, points_total, len(sketches)),
        out_shape=(
            jax.ShapeDtypeStruct((own_rows, columns), f32),
            jax.ShapeDtypeStruct((columns, columns), f32),
        ),
        in_specs=[vmem] * (2 + len(sketches)),
        out_specs=(vmem, vmem),
        name="back",
    )(part, other, *sketches)
    return basis, factor


def solution(mesh):
    in_specs = (P("tm", "pts"), P(), P("pts"), P("tm", None))
    out_specs = (P(("pts", "tm"), None), P())
    return jax.shard_map(
        on_device, mesh=mesh, in_specs=in_specs, out_specs=out_specs, check_vma=False
    )
```

```python
import functools
import math

import jax
import jax.numpy as jnp
import numpy as np
from jax import lax
from jax.experimental import pallas as pl
from jax.experimental.pallas import tpu as pltpu
from jax.sharding import PartitionSpec as P


HARM = 8
SUB = 8
AXES = ("tm", "pts")
HI = lax.Precision.HIGHEST

year_days = 365.25


def harmonic_filter(days_total):
    phase_base = np.arange(days_total).astype(np.float32)
    columns = [np.ones_like(phase_base)]
    for order in range(1, HARM + 1):
        phase = np.float32(2.0 * math.pi * order / year_days) * phase_base
        columns.append(np.cos(phase.astype(np.float64)))
        columns.append(np.sin(phase.astype(np.float64)))
    table = np.stack(columns, 0).astype(np.float32).astype(np.float64)
    low = np.linalg.cholesky(table @ table.T)
    rows = np.linalg.solve(low, table)
    padded = -(-rows.shape[0] // SUB) * SUB
    rows = np.concatenate([rows, np.zeros((padded - rows.shape[0], days_total))], 0)
    return rows.astype(np.float32)


def nn(a, b):
    return jnp.dot(a, b, precision=HI, preferred_element_type=jnp.float32)


def nt(a, b):
    return lax.dot_general(
        a, b, (((1,), (1,)), ((), ())), precision=HI, preferred_element_type=jnp.float32
    )


def tn(a, b):
    return lax.dot_general(
        a, b, (((0,), (0,)), ((), ())), precision=HI, preferred_element_type=jnp.float32
    )


def swap(value, bit):
    total = lax.axis_size("tm") * lax.axis_size("pts")
    return lax.ppermute(value, AXES, [(i, i ^ bit) for i in range(total)])


def front_kernel(start, own_rows, tm_count, first, last, *refs):
    refs = list(refs)
    take = lambda n: [refs.pop(0) for _ in range(n)]
    (days_ref, thr_ref, bin_ref, filt_ref, filt_t_ref, test_ref) = take(6)
    recv_refs = take(tm_count - 1)
    half_refs = take(2 * (tm_count - 1))
    acc_ref = None if first else take(1)[0]
    sketch_ref = take(1)[0]
    outs = take(2) if last else take(1)
    own_ref, table_ref, sem = take(3)
    width = own_ref.shape[1]
    days_local = own_ref.shape[0]
    place = lax.axis_index("tm")
    low = lax.axis_index("pts") % 2
    at = pl.multiple_of(place * own_rows + start, math.gcd(own_rows, start) if start else own_rows)
    copy = pltpu.make_async_copy(days_ref.at[:, pl.ds(at, width)], own_ref, sem)
    copy.start()
    table_ref[:days_local, :] = test_ref[...]
    half = days_local // 2
    for k in range(tm_count - 1):
        base = days_local * (k + 1)
        table_ref[pl.ds(pl.multiple_of(base + low * half, half), half), :] = half_refs[2 * k][...]
        table_ref[pl.ds(pl.multiple_of(base + (1 - low) * half, half), half), :] = half_refs[2 * k + 1][...]
    bins = bin_ref[:, pl.ds(at, width)]
    count = thr_ref.shape[0]
    entry = lax.broadcasted_iota(jnp.int32, (count, width), 0)
    level = jnp.sum(jnp.where(entry == bins, thr_ref[...], 0.0), axis=0, keepdims=True)
    copy.wait()
    series = [own_ref[...]] + [r[...] for r in recv_refs]
    proj = nn(filt_ref[place], series[0])
    for k in range(1, tm_count):
        proj = proj + nn(filt_ref[place ^ k], series[k])
    excess = [
        jnp.maximum(series[k] - nn(filt_t_ref[place ^ k], proj) - level, 0.0)
        for k in range(tm_count)
    ]
    sketch = tn(jnp.concatenate(excess, 0), table_ref[...])
    sketch_ref[...] = sketch
    cross = tn(sketch, sketch)
    if not first:
        cross = cross + acc_ref[...]
    if not last:
        outs[0][...] = cross
        return
    kept_ref, sent_ref = outs
    tile = cross.shape[0] // 2
    row = lax.broadcasted_iota(jnp.int32, (tile, tile), 0)
    col = lax.broadcasted_iota(jnp.int32, (tile, tile), 1)
    second = cross[tile:, tile:]
    ends = jnp.where(row >= col, cross[:tile, :tile], second)
    side = cross[tile:, :tile]
    diag = jnp.broadcast_to(
        jnp.sum(jnp.where(row == col, second, 0.0), axis=0, keepdims=True), (SUB, tile)
    )
    kept_ref[:tile, :] = jnp.where(low == 0, ends, side)
    sent_ref[:tile, :] = jnp.where(low == 0, side, ends)
    kept_ref[tile:, :] = diag
    sent_ref[tile:, :] = diag


def over_lanes(value, col, tile):
    return jnp.broadcast_to(value[:, col:col + 1], (SUB, tile))


def over_rows(value, row, tile):
    return jnp.broadcast_to(value[row:row + 1, :], (SUB, tile))


def panel(blocks):
    count = len(blocks)
    blocks = list(blocks)
    tile = count * SUB
    lane = lax.broadcasted_iota(jnp.int32, (SUB, tile), 1)
    row = lax.broadcasted_iota(jnp.int32, (SUB, tile), 0)
    upper, inverse = [], []
    for i in range(count):
        first = SUB * i
        own = blocks[i]
        cols = [over_lanes(own, first + k, tile) for k in range(SUB)]
        e = {(j, k): over_rows(cols[k], j, tile) for k in range(SUB) for j in range(k + 1)}
        inside = (lane >= first) & (lane < first + SUB)
        later = {
            t: [over_lanes(blocks[t], first + k, tile) for k in range(SUB)]
            for t in range(i + 1, count)
        }
        rows = [
            jnp.where(inside, jnp.where(lane == first + j, 1.0, 0.0), over_rows(own, j, tile))
            for j in range(SUB)
        ]
        for j in range(SUB):
            s = lax.rsqrt(e[j, j])
            fac = {k: e[j, k] * s for k in range(j + 1, SUB)}
            e[j, j] = e[j, j] * s
            rows[j] = rows[j] * s
            for t in later:
                later[t][j] = later[t][j] * s
            for k in range(j + 1, SUB):
                e[j, k] = fac[k]
                for m in range(k, SUB):
                    e[k, m] = e[k, m] - fac[k] * fac[m]
                rows[k] = rows[k] - fac[k] * rows[j]
                for t in later:
                    later[t][k] = later[t][k] - fac[k] * later[t][j]
        for t in later:
            terms = [later[t][j] * rows[j] for j in range(SUB)]
            while len(terms) > 1:
                terms = [terms[q] + terms[q + 1] for q in range(0, len(terms), 2)]
            blocks[t] = jnp.where(inside, 0.0, blocks[t]) - terms[0]
        up = jnp.zeros((SUB, tile), jnp.float32)
        inv = up
        for j in range(SUB):
            line = jnp.where(lane >= first + SUB, rows[j], 0.0)
            for k in range(j, SUB):
                line = jnp.where(lane == first + k, e[j, k], line)
            up = jnp.where(row == j, line, up)
            inv = jnp.where(row == j, rows[j], inv)
        upper.append(up)
        inverse.append(jnp.where(lane < first + SUB, inv, 0.0))
    return jnp.concatenate(upper, 0), jnp.concatenate(inverse, 0)


def back_kernel(points_total, chunks, part_ref, other_ref, *refs):
    sketch_refs = refs[:chunks]
    basis_ref, factor_ref = refs[chunks:]
    tile = part_ref.shape[1]
    low = lax.axis_index("pts") % 2
    part = part_ref[...] / points_total
    other = other_ref[...] / points_total
    ends = jnp.where(low == 0, part[:tile], other[:tile])
    side = jnp.where(low == 0, other[:tile], part[:tile])
    diag = jnp.where(low == 0, other[tile:tile + 1], part[tile:tile + 1])
    row = lax.broadcasted_iota(jnp.int32, (tile, tile), 0)
    col = lax.broadcasted_iota(jnp.int32, (tile, tile), 1)
    ends_t = ends.T
    side_t = side.T
    split = lambda a: [a[SUB * t:SUB * (t + 1), :] for t in range(tile // SUB)]
    up, inv1 = panel(split(jnp.where(row >= col, ends, ends_t)))
    factor_ref[:tile, :tile] = up
    factor_ref[tile:, :tile] = jnp.zeros((tile, tile), jnp.float32)
    right = nn(inv1, side_t)
    right_t = nt(side, inv1)
    factor_ref[:tile, tile:] = right
    rest = jnp.where(row < col, ends, jnp.where(row == col, diag, ends_t)) - nn(right_t, right)
    up, inv2 = panel(split(rest))
    factor_ref[tile:, tile:] = up
    at = 0
    for ref in sketch_refs:
        size = ref.shape[0]
        left = nt(ref[:, :tile], inv1)
        basis_ref[at:at + size, :tile] = left
        basis_ref[at:at + size, tile:] = nt(ref[:, tile:] - nn(left, right), inv2)
        at += size


def chunk_widths(own_rows):
    last = own_rows // 4
    if last % 128:
        return [own_rows]
    return [own_rows - last, last]


def on_device(precip, thresholds, bin_index, test_matrix):
    tm_count = lax.axis_size("tm")
    pts_count = lax.axis_size("pts")
    place = lax.axis_index("tm")
    low = lax.axis_index("pts") % 2
    days_local, points_local = precip.shape
    columns = test_matrix.shape[1]
    tile = columns // 2
    own_rows = points_local // tm_count
    days_total = days_local * tm_count
    points_total = points_local * pts_count
    f32 = jnp.float32

    rows = harmonic_filter(days_total)
    filt = rows.reshape(rows.shape[0], tm_count, days_local).transpose(1, 0, 2)
    filt_t = jnp.asarray(filt.transpose(0, 2, 1))
    filt = jnp.asarray(filt)
    thr = thresholds[:, None]
    bins = bin_index[None, :]

    half = days_local // 2
    mine = lax.dynamic_slice_in_dim(test_matrix, low * half, half, 0)
    halves = []
    for k in range(1, tm_count):
        halves.append(swap(mine, k * pts_count))
    halves = [h for got in halves for h in (got, swap(got, 1))]

    vmem = pl.BlockSpec(memory_space=pltpu.VMEM)
    start = 0
    widths = chunk_widths(own_rows)
    received = []
    for width in widths:
        received.append(
            [
                swap(
                    lax.dynamic_slice_in_dim(precip, (place ^ k) * own_rows + start, width, 1),
                    k * pts_count,
                )
                for k in range(1, tm_count)
            ]
        )
        start += width

    sketches = []
    cross = None
    start = 0
    for index, width in enumerate(widths):
        first, last = index == 0, index == len(widths) - 1
        operands = [precip, thr, bins, filt, filt_t, test_matrix] + received[index] + halves
        specs = [pl.BlockSpec(memory_space=pl.ANY)] + [vmem] * (len(operands) - 1)
        if not first:
            operands.append(cross)
            specs.append(vmem)
        shapes = [jax.ShapeDtypeStruct((width, columns), f32)]
        if last:
            shapes += [jax.ShapeDtypeStruct((tile + SUB, tile), f32)] * 2
        else:
            shapes += [jax.ShapeDtypeStruct((columns, columns), f32)]
        out = pl.pallas_call(
            functools.partial(front_kernel, start, own_rows, tm_count, first, last),
            out_shape=shapes,
            in_specs=specs,
            out_specs=[vmem] * len(shapes),
            scratch_shapes=[
                pltpu.VMEM((days_local, width), f32),
                pltpu.VMEM((days_total, columns), f32),
                pltpu.SemaphoreType.DMA,
            ],
            cost_estimate=pl.CostEstimate(
                flops=12 * width * columns * (days_total + columns),
                bytes_accessed=4 * days_total * (width + columns),
                transcendentals=0,
            ),
            compiler_params=pltpu.CompilerParams(vmem_limit_bytes=16 << 20),
            name=f"front{index}",
        )(*operands)
        sketches.append(out[0])
        cross = out[1]
        start += width
    kept, sent = out[1], out[2]

    part = kept + swap(sent, 1)
    bit = 2
    while bit < tm_count * pts_count:
        part = part + swap(part, bit)
        bit *= 2
    other = swap(part, 1)

    basis, factor = pl.pallas_call(
        functools.partial(back_kernel, points_total, len(sketches)),
        out_shape=(
            jax.ShapeDtypeStruct((own_rows, columns), f32),
            jax.ShapeDtypeStruct((columns, columns), f32),
        ),
        in_specs=[vmem] * (2 + len(sketches)),
        out_specs=(vmem, vmem),
        compiler_params=pltpu.CompilerParams(vmem_limit_bytes=16 << 20),
        name="back",
    )(part, other, *sketches)
    return basis, factor


def solution(mesh):
    in_specs = (P("tm", "pts"), P(), P("pts"), P("tm", None))
    out_specs = (P(("pts", "tm"), None), P())
    return jax.shard_map(
        on_device, mesh=mesh, in_specs=in_specs, out_specs=out_specs, check_vma=False
    )
```

```python
import functools
import math

import jax
import jax.numpy as jnp
import numpy as np
from jax import lax
from jax.experimental import pallas as pl
from jax.experimental.pallas import tpu as pltpu
from jax.sharding import PartitionSpec as P


HARM = 8
SUB = 8
AXES = ("tm", "pts")
HI = lax.Precision.HIGHEST

year_days = 365.25


def harmonic_filter(days_total):
    phase_base = np.arange(days_total).astype(np.float32)
    columns = [np.ones_like(phase_base)]
    for order in range(1, HARM + 1):
        phase = np.float32(2.0 * math.pi * order / year_days) * phase_base
        columns.append(np.cos(phase.astype(np.float64)))
        columns.append(np.sin(phase.astype(np.float64)))
    table = np.stack(columns, 0).astype(np.float32).astype(np.float64)
    low = np.linalg.cholesky(table @ table.T)
    rows = np.linalg.solve(low, table)
    padded = -(-rows.shape[0] // SUB) * SUB
    rows = np.concatenate([rows, np.zeros((padded - rows.shape[0], days_total))], 0)
    return rows.astype(np.float32)


def nn(a, b):
    return jnp.dot(a, b, precision=HI, preferred_element_type=jnp.float32)


def nt(a, b):
    return lax.dot_general(
        a, b, (((1,), (1,)), ((), ())), precision=HI, preferred_element_type=jnp.float32
    )


def tn(a, b):
    return lax.dot_general(
        a, b, (((0,), (0,)), ((), ())), precision=HI, preferred_element_type=jnp.float32
    )


def swap(value, bit, odd_bit=None):
    total = lax.axis_size("tm") * lax.axis_size("pts")
    odd_bit = bit if odd_bit is None else odd_bit
    return lax.ppermute(
        value, AXES, [(i, i ^ (odd_bit if i % 2 else bit)) for i in range(total)]
    )


def cut_kernel(widths, own_rows, tm_count, days_ref, *refs):
    piece_refs, sem = refs[:-1], refs[-1]
    place = lax.axis_index("tm")
    copies = []
    start = 0
    for width in widths:
        for k in range(1, tm_count):
            at = pl.multiple_of((place ^ k) * own_rows + start, math.gcd(own_rows, start))
            n = len(copies)
            copies.append(
                pltpu.make_async_copy(days_ref.at[:, pl.ds(at, width)], piece_refs[n], sem.at[n])
            )
        start += width
    for copy in copies:
        copy.start()
    for copy in copies:
        copy.wait()


def front_kernel(start, width, own_rows, tm_count, earlier, with_acc, with_cross, last, *refs):
    refs = list(refs)
    take = lambda n: [refs.pop(0) for _ in range(n)]
    days_ref, thr_ref, bin_ref, filt_ref, test_ref = take(5)
    recv_refs = take(tm_count - 1)
    half_refs = take(2 * (tm_count - 1))
    earlier_refs = take(earlier)
    acc_refs = take(1 if with_acc else 0)
    sketch_ref = take(1)[0]
    outs = take(2 if last else int(with_cross))
    table_ref = take(1)[0]
    days_local = days_ref.shape[0]
    place = lax.axis_index("tm")
    low = lax.axis_index("pts") % 2
    at = pl.multiple_of(place * own_rows + start, math.gcd(own_rows, start))
    table_ref[:days_local, :] = test_ref[...]
    half = days_local // 2
    for k in range(tm_count - 1):
        base = days_local * (k + 1)
        table_ref[pl.ds(pl.multiple_of(base + low * half, half), half), :] = half_refs[2 * k][...]
        table_ref[pl.ds(pl.multiple_of(base + (1 - low) * half, half), half), :] = half_refs[2 * k + 1][...]
    bins = bin_ref[:, pl.ds(at, width)]
    count = thr_ref.shape[0]
    entry = lax.broadcasted_iota(jnp.int32, (count, width), 0)
    level = jnp.sum(jnp.where(entry == bins, thr_ref[...], 0.0), axis=0, keepdims=True)
    series = [days_ref[:, pl.ds(at, width)]] + [r[...] for r in recv_refs]
    proj = nn(filt_ref[place], series[0])
    for k in range(1, tm_count):
        proj = proj + nn(filt_ref[place ^ k], series[k])
    excess = [
        jnp.maximum(series[k] - tn(filt_ref[place ^ k], proj) - level, 0.0)
        for k in range(tm_count)
    ]
    sketch = tn(jnp.concatenate(excess, 0), table_ref[...])
    sketch_ref[...] = sketch
    if not with_cross:
        return
    whole = jnp.concatenate([r[...] for r in earlier_refs] + [sketch], 0)
    cross = tn(whole, whole)
    for ref in acc_refs:
        cross = cross + ref[...]
    if not last:
        outs[0][...] = cross
        return
    kept_ref, sent_ref = outs
    tile = cross.shape[0] // 2
    row = lax.broadcasted_iota(jnp.int32, (tile, tile), 0)
    col = lax.broadcasted_iota(jnp.int32, (tile, tile), 1)
    second = cross[tile:, tile:]
    ends = jnp.where(row >= col, cross[:tile, :tile], second)
    side = cross[tile:, :tile]
    diag = jnp.broadcast_to(
        jnp.sum(jnp.where(row == col, second, 0.0), axis=0, keepdims=True), (SUB, tile)
    )
    kept_ref[:tile, :] = jnp.where(low == 0, ends, side)
    sent_ref[:tile, :] = jnp.where(low == 0, side, ends)
    kept_ref[tile:, :] = diag
    sent_ref[tile:, :] = diag


def over_lanes(value, col, tile):
    return jnp.broadcast_to(value[:, col:col + 1], (SUB, tile))


def over_rows(value, row, tile):
    return jnp.broadcast_to(value[row:row + 1, :], (SUB, tile))


def panel(blocks):
    count = len(blocks)
    blocks = list(blocks)
    tile = count * SUB
    lane = lax.broadcasted_iota(jnp.int32, (SUB, tile), 1)
    row = lax.broadcasted_iota(jnp.int32, (SUB, tile), 0)
    upper, inverse = [], []
    for i in range(count):
        first = SUB * i
        own = blocks[i]
        cols = [over_lanes(own, first + k, tile) for k in range(SUB)]
        e = {(j, k): over_rows(cols[k], j, tile) for k in range(SUB) for j in range(k + 1)}
        inside = (lane >= first) & (lane < first + SUB)
        later = {
            t: [over_lanes(blocks[t], first + k, tile) for k in range(SUB)]
            for t in range(i + 1, count)
        }
        rows = [
            jnp.where(inside, jnp.where(lane == first + j, 1.0, 0.0), over_rows(own, j, tile))
            for j in range(SUB)
        ]
        for j in range(SUB):
            s = lax.rsqrt(e[j, j])
            fac = {k: e[j, k] * s for k in range(j + 1, SUB)}
            e[j, j] = e[j, j] * s
            rows[j] = rows[j] * s
            for t in later:
                later[t][j] = later[t][j] * s
            for k in range(j + 1, SUB):
                e[j, k] = fac[k]
                for m in range(k, SUB):
                    e[k, m] = e[k, m] - fac[k] * fac[m]
                rows[k] = rows[k] - fac[k] * rows[j]
                for t in later:
                    later[t][k] = later[t][k] - fac[k] * later[t][j]
        for t in later:
            terms = [later[t][j] * rows[j] for j in range(SUB)]
            while len(terms) > 1:
                terms = [terms[q] + terms[q + 1] for q in range(0, len(terms), 2)]
            blocks[t] = jnp.where(inside, 0.0, blocks[t]) - terms[0]
        up = jnp.zeros((SUB, tile), jnp.float32)
        inv = up
        for j in range(SUB):
            line = jnp.where(lane >= first + SUB, rows[j], 0.0)
            for k in range(j, SUB):
                line = jnp.where(lane == first + k, e[j, k], line)
            up = jnp.where(row == j, line, up)
            inv = jnp.where(row == j, rows[j], inv)
        upper.append(up)
        inverse.append(jnp.where(lane < first + SUB, inv, 0.0))
    return jnp.concatenate(upper, 0), jnp.concatenate(inverse, 0)


def back_kernel(points_total, chunks, part_ref, other_ref, *refs):
    sketch_refs = refs[:chunks]
    basis_ref, factor_ref = refs[chunks:]
    tile = part_ref.shape[1]
    low = lax.axis_index("pts") % 2
    part = part_ref[...] / points_total
    other = other_ref[...] / points_total
    ends = jnp.where(low == 0, part[:tile], other[:tile])
    side = jnp.where(low == 0, other[:tile], part[:tile])
    diag = jnp.where(low == 0, other[tile:tile + 1], part[tile:tile + 1])
    row = lax.broadcasted_iota(jnp.int32, (tile, tile), 0)
    col = lax.broadcasted_iota(jnp.int32, (tile, tile), 1)
    ends_t = ends.T
    side_t = side.T
    split = lambda a: [a[SUB * t:SUB * (t + 1), :] for t in range(tile // SUB)]
    up, inv1 = panel(split(jnp.where(row >= col, ends, ends_t)))
    factor_ref[:tile, :tile] = up
    factor_ref[tile:, :tile] = jnp.zeros((tile, tile), jnp.float32)
    right = nn(inv1, side_t)
    right_t = nt(side, inv1)
    factor_ref[:tile, tile:] = right
    rest = jnp.where(row < col, ends, jnp.where(row == col, diag, ends_t)) - nn(right_t, right)
    up, inv2 = panel(split(rest))
    factor_ref[tile:, tile:] = up
    at = 0
    for ref in sketch_refs:
        size = ref.shape[0]
        left = nt(ref[:, :tile], inv1)
        basis_ref[at:at + size, :tile] = left
        basis_ref[at:at + size, tile:] = nt(ref[:, tile:] - nn(left, right), inv2)
        at += size


def chunk_widths(own_rows):
    step = own_rows // 4
    if step % 128:
        return [own_rows]
    return [2 * step, step, step]


def on_device(precip, thresholds, bin_index, test_matrix):
    tm_count = lax.axis_size("tm")
    pts_count = lax.axis_size("pts")
    low = lax.axis_index("pts") % 2
    days_local, points_local = precip.shape
    columns = test_matrix.shape[1]
    tile = columns // 2
    own_rows = points_local // tm_count
    days_total = days_local * tm_count
    points_total = points_local * pts_count
    f32 = jnp.float32

    rows = harmonic_filter(days_total)
    filt = rows.reshape(rows.shape[0], tm_count, days_local).transpose(1, 0, 2)
    filt = jnp.asarray(filt)
    thr = thresholds[:, None]
    bins = bin_index[None, :]

    vmem = pl.BlockSpec(memory_space=pltpu.VMEM)
    widths = chunk_widths(own_rows)
    half = days_local // 2
    mine = lax.dynamic_slice_in_dim(test_matrix, low * half, half, 0)
    shapes = [
        jax.ShapeDtypeStruct((days_local, width), f32)
        for width in widths
        for _ in range(tm_count - 1)
    ]
    pieces = pl.pallas_call(
        functools.partial(cut_kernel, widths, own_rows, tm_count),
        out_shape=shapes,
        in_specs=[pl.BlockSpec(memory_space=pl.ANY)],
        out_specs=[vmem] * len(shapes),
        scratch_shapes=[pltpu.SemaphoreType.DMA((len(shapes),))],
        compiler_params=pltpu.CompilerParams(vmem_limit_bytes=4 << 20),
        name="cut",
    )(precip)
    sends = [("rows", mine, k) for k in range(1, tm_count)]
    for n in range(len(widths)):
        sends += [("points", pieces[n * (tm_count - 1) + k - 1], k) for k in range(1, tm_count)]
    came = []
    for _, value, k in sends:
        came.append(swap(value, k * pts_count))
    halves, came = came[:tm_count - 1], came[tm_count - 1:]
    received = [came[n * (tm_count - 1):(n + 1) * (tm_count - 1)] for n in range(len(widths))]
    halves = [h for got in halves for h in (got, swap(got, 1))]

    sketches, waiting = [], []
    cross = None
    start = 0
    for index, width in enumerate(widths):
        last = index == len(widths) - 1
        with_cross = last or index == 0
        if sketches:
            received[index], sketches[-1] = lax.optimization_barrier((received[index], sketches[-1]))
        operands = [precip, thr, bins, filt, test_matrix] + received[index] + halves
        operands += waiting if with_cross else []
        operands += [cross] if with_cross and cross is not None else []
        shapes = [jax.ShapeDtypeStruct((width, columns), f32)]
        if last:
            shapes += [jax.ShapeDtypeStruct((tile + SUB, tile), f32)] * 2
        elif with_cross:
            shapes += [jax.ShapeDtypeStruct((columns, columns), f32)]
        out = pl.pallas_call(
            functools.partial(
                front_kernel,
                start,
                width,
                own_rows,
                tm_count,
                len(waiting) if with_cross else 0,
                with_cross and cross is not None,
                with_cross,
                last,
            ),
            out_shape=shapes,
            in_specs=[vmem] * len(operands),
            out_specs=[vmem] * len(shapes),
            scratch_shapes=[pltpu.VMEM((days_total, columns), f32)],
            cost_estimate=pl.CostEstimate(
                flops=12 * width * columns * (days_total + columns),
                bytes_accessed=4 * days_total * (width + columns),
                transcendentals=0,
            ),
            compiler_params=pltpu.CompilerParams(vmem_limit_bytes=16 << 20),
        )(*operands)
        sketches.append(out[0])
        if with_cross:
            waiting = []
            cross = out[1]
        else:
            waiting.append(out[0])
        start += width
    kept, sent = out[1], out[2]

    part = kept + swap(sent, 1)
    bits = [1 << n for n in range(1, (tm_count * pts_count).bit_length() - 1)]
    shift = (len(bits) + 1) // 2
    for n in range(len(bits)):
        part = part + swap(part, bits[n], bits[(n + shift) % len(bits)])
    other = swap(part, 1)

    basis, factor = pl.pallas_call(
        functools.partial(back_kernel, points_total, len(sketches)),
        out_shape=(
            jax.ShapeDtypeStruct((own_rows, columns), f32),
            jax.ShapeDtypeStruct((columns, columns), f32),
        ),
        in_specs=[vmem] * (2 + len(sketches)),
        out_specs=(vmem, vmem),
        compiler_params=pltpu.CompilerParams(vmem_limit_bytes=16 << 20),
        name="back",
    )(part, other, *sketches)
    return basis, factor


def solution(mesh):
    in_specs = (P("tm", "pts"), P(), P("pts"), P("tm", None))
    out_specs = (P(("pts", "tm"), None), P())

    return jax.shard_map(
        on_device, mesh=mesh, in_specs=in_specs, out_specs=out_specs, check_vma=False
    )
```

```python
import functools
import math

import jax
import jax.numpy as jnp
import numpy as np
from jax import lax
from jax.experimental import pallas as pl
from jax.experimental.pallas import tpu as pltpu
from jax.sharding import PartitionSpec as P


HARM = 8
SUB = 8
AXES = ("tm", "pts")
HI = lax.Precision.HIGHEST

year_days = 365.25


def harmonic_filter(days_total):
    phase_base = np.arange(days_total).astype(np.float32)
    columns = [np.ones_like(phase_base)]
    for order in range(1, HARM + 1):
        phase = np.float32(2.0 * math.pi * order / year_days) * phase_base
        columns.append(np.cos(phase.astype(np.float64)))
        columns.append(np.sin(phase.astype(np.float64)))
    table = np.stack(columns, 0).astype(np.float32).astype(np.float64)
    low = np.linalg.cholesky(table @ table.T)
    rows = np.linalg.solve(low, table)
    padded = -(-rows.shape[0] // SUB) * SUB
    rows = np.concatenate([rows, np.zeros((padded - rows.shape[0], days_total))], 0)
    return rows.astype(np.float32)


def nn(a, b):
    return jnp.dot(a, b, precision=HI, preferred_element_type=jnp.float32)


def nt(a, b):
    return lax.dot_general(
        a, b, (((1,), (1,)), ((), ())), precision=HI, preferred_element_type=jnp.float32
    )


def tn(a, b):
    return lax.dot_general(
        a, b, (((0,), (0,)), ((), ())), precision=HI, preferred_element_type=jnp.float32
    )


def swap(value, bit, odd_bit=None):
    total = lax.axis_size("tm") * lax.axis_size("pts")
    odd_bit = bit if odd_bit is None else odd_bit
    return lax.ppermute(
        value, AXES, [(i, i ^ (odd_bit if i % 2 else bit)) for i in range(total)]
    )


def partners(bits):
    return list(bits) + ([bits[0] ^ bits[1]] if len(bits) == 2 else [])


def partners_order(groups):
    return groups[::-1] if len({len(g) for g in groups}) == 1 else groups


def cut_kernel(widths, own_rows, tm_count, days_ref, *refs):
    piece_refs, sem = refs[:-1], refs[-1]
    place = lax.axis_index("tm")
    copies = []
    start = 0
    for width in widths:
        for k in range(1, tm_count):
            at = pl.multiple_of((place ^ k) * own_rows + start, math.gcd(own_rows, start))
            n = len(copies)
            copies.append(
                pltpu.make_async_copy(days_ref.at[:, pl.ds(at, width)], piece_refs[n], sem.at[n])
            )
        start += width
    for copy in copies:
        copy.start()
    for copy in copies:
        copy.wait()


def front_kernel(start, width, own_rows, tm_count, earlier, with_acc, with_cross, last, *refs):
    refs = list(refs)
    take = lambda n: [refs.pop(0) for _ in range(n)]
    days_ref, thr_ref, bin_ref, filt_ref, test_ref = take(5)
    recv_refs = take(tm_count - 1)
    half_refs = take(2 * (tm_count - 1))
    earlier_refs = take(earlier)
    acc_refs = take(1 if with_acc else 0)
    sketch_ref = take(1)[0]
    outs = take(2 if last else int(with_cross))
    table_ref = take(1)[0]
    days_local = days_ref.shape[0]
    place = lax.axis_index("tm")
    low = lax.axis_index("pts") % 2
    at = pl.multiple_of(place * own_rows + start, math.gcd(own_rows, start))
    table_ref[:days_local, :] = test_ref[...]
    half = days_local // 2
    for k in range(tm_count - 1):
        base = days_local * (k + 1)
        table_ref[pl.ds(pl.multiple_of(base + low * half, half), half), :] = half_refs[2 * k][...]
        table_ref[pl.ds(pl.multiple_of(base + (1 - low) * half, half), half), :] = half_refs[2 * k + 1][...]
    bins = bin_ref[:, pl.ds(at, width)]
    count = thr_ref.shape[0]
    entry = lax.broadcasted_iota(jnp.int32, (count, width), 0)
    level = jnp.sum(jnp.where(entry == bins, thr_ref[...], 0.0), axis=0, keepdims=True)
    series = [days_ref[:, pl.ds(at, width)]] + [r[...] for r in recv_refs]
    proj = nn(filt_ref[place], series[0])
    for k in range(1, tm_count):
        proj = proj + nn(filt_ref[place ^ k], series[k])
    excess = [
        jnp.maximum(series[k] - tn(filt_ref[place ^ k], proj) - level, 0.0)
        for k in range(tm_count)
    ]
    sketch = tn(jnp.concatenate(excess, 0), table_ref[...])
    sketch_ref[...] = sketch
    if not with_cross:
        return
    whole = jnp.concatenate([r[...] for r in earlier_refs] + [sketch], 0)
    cross = tn(whole, whole)
    for ref in acc_refs:
        cross = cross + ref[...]
    if not last:
        outs[0][...] = cross
        return
    kept_ref, sent_ref = outs
    tile = cross.shape[0] // 2
    row = lax.broadcasted_iota(jnp.int32, (tile, tile), 0)
    col = lax.broadcasted_iota(jnp.int32, (tile, tile), 1)
    second = cross[tile:, tile:]
    ends = jnp.where(row >= col, cross[:tile, :tile], second)
    side = cross[tile:, :tile]
    diag = jnp.broadcast_to(
        jnp.sum(jnp.where(row == col, second, 0.0), axis=0, keepdims=True), (SUB, tile)
    )
    kept_ref[:tile, :] = jnp.where(low == 0, ends, side)
    sent_ref[:tile, :] = jnp.where(low == 0, side, ends)
    kept_ref[tile:, :] = diag
    sent_ref[tile:, :] = diag


def over_lanes(value, col, tile):
    return jnp.broadcast_to(value[:, col:col + 1], (SUB, tile))


def over_rows(value, row, tile):
    return jnp.broadcast_to(value[row:row + 1, :], (SUB, tile))


def tree(terms):
    while len(terms) > 1:
        terms = [terms[q] + terms[q + 1] for q in range(0, len(terms), 2)]
    return terms[0]


def panel(blocks):
    count = len(blocks)
    blocks = list(blocks)
    tile = count * SUB
    lane = lax.broadcasted_iota(jnp.int32, (SUB, tile), 1)
    row = lax.broadcasted_iota(jnp.int32, (SUB, tile), 0)
    upper, inverse = [], []
    for i in range(count):
        first = SUB * i
        own = blocks[i]
        cols = [over_lanes(own, first + k, tile) for k in range(SUB)] if i == 0 else ahead
        e = {(j, k): over_rows(cols[k], j, tile) for k in range(SUB) for j in range(k + 1)}
        inside = (lane >= first) & (lane < first + SUB)
        later = {
            t: [over_lanes(blocks[t], first + k, tile) for k in range(SUB)]
            for t in range(i + 1, count)
        }
        if i + 1 < count:
            ahead = [over_lanes(blocks[i + 1], first + SUB + k, tile) for k in range(SUB)]
        rows = [
            jnp.where(inside, jnp.where(lane == first + j, 1.0, 0.0), over_rows(own, j, tile))
            for j in range(SUB)
        ]
        for j in range(SUB):
            s = lax.rsqrt(e[j, j])
            fac = {k: e[j, k] * s for k in range(j + 1, SUB)}
            e[j, j] = e[j, j] * s
            rows[j] = rows[j] * s
            for t in later:
                later[t][j] = later[t][j] * s
            for k in range(j + 1, SUB):
                e[j, k] = fac[k]
                for m in range(k, SUB):
                    e[k, m] = e[k, m] - fac[k] * fac[m]
                rows[k] = rows[k] - fac[k] * rows[j]
                for t in later:
                    later[t][k] = later[t][k] - fac[k] * later[t][j]
        if i + 1 < count:
            nxt = later[i + 1]
            for k in range(SUB):
                ahead[k] = ahead[k] - tree([nxt[j] * over_rows(nxt[j], k, tile) for j in range(SUB)])
        for t in later:
            update = tree([later[t][j] * rows[j] for j in range(SUB)])
            blocks[t] = jnp.where(inside, 0.0, blocks[t]) - update
        up = jnp.zeros((SUB, tile), jnp.float32)
        inv = up
        for j in range(SUB):
            line = jnp.where(lane >= first + SUB, rows[j], 0.0)
            for k in range(j, SUB):
                line = jnp.where(lane == first + k, e[j, k], line)
            up = jnp.where(row == j, line, up)
            inv = jnp.where(row == j, rows[j], inv)
        upper.append(up)
        inverse.append(jnp.where(lane < first + SUB, inv, 0.0))
    return jnp.concatenate(upper, 0), jnp.concatenate(inverse, 0)


def back_kernel(points_total, chunks, part_ref, other_ref, *refs):
    sketch_refs = refs[:chunks]
    basis_ref, factor_ref = refs[chunks:]
    tile = part_ref.shape[1]
    low = lax.axis_index("pts") % 2
    part = part_ref[...] / points_total
    other = other_ref[...] / points_total
    ends = jnp.where(low == 0, part[:tile], other[:tile])
    side = jnp.where(low == 0, other[:tile], part[:tile])
    diag = jnp.where(low == 0, other[tile:tile + 1], part[tile:tile + 1])
    row = lax.broadcasted_iota(jnp.int32, (tile, tile), 0)
    col = lax.broadcasted_iota(jnp.int32, (tile, tile), 1)
    ends_t = ends.T
    side_t = side.T
    split = lambda a: [a[SUB * t:SUB * (t + 1), :] for t in range(tile // SUB)]
    up, inv1 = panel(split(jnp.where(row >= col, ends, ends_t)))
    factor_ref[:tile, :tile] = up
    factor_ref[tile:, :tile] = jnp.zeros((tile, tile), jnp.float32)
    right = nn(inv1, side_t)
    right_t = nt(side, inv1)
    factor_ref[:tile, tile:] = right
    rest = jnp.where(row < col, ends, jnp.where(row == col, diag, ends_t)) - nn(right_t, right)
    up, inv2 = panel(split(rest))
    factor_ref[tile:, tile:] = up
    at = 0
    for ref in sketch_refs:
        size = ref.shape[0]
        left = nt(ref[:, :tile], inv1)
        basis_ref[at:at + size, :tile] = left
        basis_ref[at:at + size, tile:] = nt(ref[:, tile:] - nn(left, right), inv2)
        at += size


def chunk_widths(own_rows):
    step = own_rows // 4
    if step % 128:
        return [own_rows]
    return [2 * step, step, step]


def on_device(precip, thresholds, bin_index, test_matrix):
    tm_count = lax.axis_size("tm")
    pts_count = lax.axis_size("pts")
    low = lax.axis_index("pts") % 2
    days_local, points_local = precip.shape
    columns = test_matrix.shape[1]
    tile = columns // 2
    own_rows = points_local // tm_count
    days_total = days_local * tm_count
    points_total = points_local * pts_count
    f32 = jnp.float32

    rows = harmonic_filter(days_total)
    filt = rows.reshape(rows.shape[0], tm_count, days_local).transpose(1, 0, 2)
    filt = jnp.asarray(filt)
    thr = thresholds[:, None]
    bins = bin_index[None, :]

    vmem = pl.BlockSpec(memory_space=pltpu.VMEM)
    widths = chunk_widths(own_rows)
    half = days_local // 2
    mine = lax.dynamic_slice_in_dim(test_matrix, low * half, half, 0)
    shapes = [
        jax.ShapeDtypeStruct((days_local, width), f32)
        for width in widths
        for _ in range(tm_count - 1)
    ]
    pieces = pl.pallas_call(
        functools.partial(cut_kernel, widths, own_rows, tm_count),
        out_shape=shapes,
        in_specs=[pl.BlockSpec(memory_space=pl.ANY)],
        out_specs=[vmem] * len(shapes),
        scratch_shapes=[pltpu.SemaphoreType.DMA((len(shapes),))],
        compiler_params=pltpu.CompilerParams(vmem_limit_bytes=4 << 20),
        name="cut",
    )(precip)
    sends = [("rows", mine, k) for k in range(1, tm_count)]
    for n in range(len(widths)):
        sends += [("points", pieces[n * (tm_count - 1) + k - 1], k) for k in range(1, tm_count)]
    came = []
    for _, value, k in sends:
        came.append(swap(value, k * pts_count))
    halves, came = came[:tm_count - 1], came[tm_count - 1:]
    received = [came[n * (tm_count - 1):(n + 1) * (tm_count - 1)] for n in range(len(widths))]
    halves = [h for got in halves for h in (got, swap(got, 1))]

    sketches, waiting = [], []
    cross = None
    start = 0
    for index, width in enumerate(widths):
        last = index == len(widths) - 1
        with_cross = last or index == 0
        if sketches:
            received[index], sketches[-1] = lax.optimization_barrier((received[index], sketches[-1]))
        operands = [precip, thr, bins, filt, test_matrix] + received[index] + halves
        operands += waiting if with_cross else []
        operands += [cross] if with_cross and cross is not None else []
        shapes = [jax.ShapeDtypeStruct((width, columns), f32)]
        if last:
            shapes += [jax.ShapeDtypeStruct((tile + SUB, tile), f32)] * 2
        elif with_cross:
            shapes += [jax.ShapeDtypeStruct((columns, columns), f32)]
        out = pl.pallas_call(
            functools.partial(
                front_kernel,
                start,
                width,
                own_rows,
                tm_count,
                len(waiting) if with_cross else 0,
                with_cross and cross is not None,
                with_cross,
                last,
            ),
            out_shape=shapes,
            in_specs=[vmem] * len(operands),
            out_specs=[vmem] * len(shapes),
            scratch_shapes=[pltpu.VMEM((days_total, columns), f32)],
            cost_estimate=pl.CostEstimate(
                flops=12 * width * columns * (days_total + columns),
                bytes_accessed=4 * days_total * (width + columns),
                transcendentals=0,
            ),
            compiler_params=pltpu.CompilerParams(vmem_limit_bytes=16 << 20),
        )(*operands)
        sketches.append(out[0])
        if with_cross:
            waiting = []
            cross = out[1]
        else:
            waiting.append(out[0])
        start += width
    kept, sent = out[1], out[2]

    part = kept + swap(sent, 1)
    bits = [1 << n for n in range(1, (tm_count * pts_count).bit_length() - 1)]
    groups = []
    while bits:
        ends = {bits.pop(0), bits.pop() if bits else 0}
        groups.append(tuple(sorted(ends)) if len(ends) == 2 and 0 not in ends else (max(ends),))
    for even, odd in zip(groups, partners_order(groups)):
        steps = list(zip(partners(even), partners(odd)))
        got = [swap(part, *pair) for pair in steps]
        while len(got) > 1:
            got = [sum(got[n:n + 2][1:], got[n]) for n in range(0, len(got), 2)]
        part = part + got[0]
    other = swap(part, 1)

    basis, factor = pl.pallas_call(
        functools.partial(back_kernel, points_total, len(sketches)),
        out_shape=(
            jax.ShapeDtypeStruct((own_rows, columns), f32),
            jax.ShapeDtypeStruct((columns, columns), f32),
        ),
        in_specs=[vmem] * (2 + len(sketches)),
        out_specs=(vmem, vmem),
        compiler_params=pltpu.CompilerParams(vmem_limit_bytes=16 << 20),
        name="back",
    )(part, other, *sketches)
    return basis, factor


def solution(mesh):
    in_specs = (P("tm", "pts"), P(), P("pts"), P("tm", None))
    out_specs = (P(("pts", "tm"), None), P())

    return jax.shard_map(
        on_device, mesh=mesh, in_specs=in_specs, out_specs=out_specs, check_vma=False
    )
```

```python
import functools
import math

import jax
import jax.numpy as jnp
import numpy as np
from jax import lax
from jax.experimental import pallas as pl
from jax.experimental.pallas import tpu as pltpu
from jax.sharding import PartitionSpec as P


HARM = 8
SUB = 8
AXES = ("tm", "pts")
QUARTERS = (0, 1, 2, 3)
HI = lax.Precision.HIGHEST

year_days = 365.25


def harmonic_filter(days_total):
    phase_base = np.arange(days_total).astype(np.float32)
    columns = [np.ones_like(phase_base)]
    for order in range(1, HARM + 1):
        phase = np.float32(2.0 * math.pi * order / year_days) * phase_base
        columns.append(np.cos(phase.astype(np.float64)))
        columns.append(np.sin(phase.astype(np.float64)))
    table = np.stack(columns, 0).astype(np.float32).astype(np.float64)
    low = np.linalg.cholesky(table @ table.T)
    rows = np.linalg.solve(low, table)
    padded = -(-rows.shape[0] // SUB) * SUB
    rows = np.concatenate([rows, np.zeros((padded - rows.shape[0], days_total))], 0)
    return rows.astype(np.float32)


def nn(a, b):
    return jnp.dot(a, b, precision=HI, preferred_element_type=jnp.float32)


def nt(a, b):
    return lax.dot_general(
        a, b, (((1,), (1,)), ((), ())), precision=HI, preferred_element_type=jnp.float32
    )


def tn(a, b):
    return lax.dot_general(
        a, b, (((0,), (0,)), ((), ())), precision=HI, preferred_element_type=jnp.float32
    )


def swap(value, bit, odd_bit=None):
    total = lax.axis_size("tm") * lax.axis_size("pts")
    odd_bit = bit if odd_bit is None else odd_bit
    return lax.ppermute(
        value, AXES, [(i, i ^ (odd_bit if i % 2 else bit)) for i in range(total)]
    )


def partners(bits):
    return list(bits) + ([bits[0] ^ bits[1]] if len(bits) == 2 else [])


def partners_order(groups):
    return groups[::-1] if len({len(g) for g in groups}) == 1 else groups


def cut_kernel(widths, own_rows, tm_count, days_ref, *refs):
    piece_refs, sem = refs[:-1], refs[-1]
    place = lax.axis_index("tm")
    copies = []
    start = 0
    for width in widths:
        for k in range(1, tm_count):
            at = pl.multiple_of((place ^ k) * own_rows + start, math.gcd(own_rows, start))
            n = len(copies)
            copies.append(
                pltpu.make_async_copy(days_ref.at[:, pl.ds(at, width)], piece_refs[n], sem.at[n])
            )
        start += width
    for copy in copies:
        copy.start()
    for copy in copies:
        copy.wait()


def front_kernel(start, width, own_rows, tm_count, earlier, with_acc, with_cross, last, *refs):
    refs = list(refs)
    take = lambda n: [refs.pop(0) for _ in range(n)]
    days_ref, thr_ref, bin_ref, filt_ref, test_ref = take(5)
    recv_refs = take(tm_count - 1)
    quarter_refs = take(len(QUARTERS) * (tm_count - 1))
    earlier_refs = take(earlier)
    acc_refs = take(1 if with_acc else 0)
    sketch_ref = take(1)[0]
    outs = take(2 if last else int(with_cross))
    table_ref = take(1)[0]
    days_local = days_ref.shape[0]
    place = lax.axis_index("tm")
    pts_place = lax.axis_index("pts")
    low = pts_place % 2
    at = pl.multiple_of(place * own_rows + start, math.gcd(own_rows, start))
    table_ref[:days_local, :] = test_ref[...]
    size = days_local // len(QUARTERS)
    for n, ref in enumerate(quarter_refs):
        peer, q = divmod(n, len(QUARTERS))
        base = days_local * (peer + 1) + ((pts_place % len(QUARTERS)) ^ QUARTERS[q]) * size
        table_ref[pl.ds(pl.multiple_of(base, size), size), :] = ref[...]
    bins = bin_ref[:, pl.ds(at, width)]
    count = thr_ref.shape[0]
    entry = lax.broadcasted_iota(jnp.int32, (count, width), 0)
    level = jnp.sum(jnp.where(entry == bins, thr_ref[...], 0.0), axis=0, keepdims=True)
    series = [days_ref[:, pl.ds(at, width)]] + [r[...] for r in recv_refs]
    proj = nn(filt_ref[place], series[0])
    for k in range(1, tm_count):
        proj = proj + nn(filt_ref[place ^ k], series[k])
    excess = [
        jnp.maximum(series[k] - tn(filt_ref[place ^ k], proj) - level, 0.0)
        for k in range(tm_count)
    ]
    sketch = tn(jnp.concatenate(excess, 0), table_ref[...])
    sketch_ref[...] = sketch
    if not with_cross:
        return
    whole = jnp.concatenate([r[...] for r in earlier_refs] + [sketch], 0)
    cross = tn(whole, whole)
    for ref in acc_refs:
        cross = cross + ref[...]
    if not last:
        outs[0][...] = cross
        return
    kept_ref, sent_ref = outs
    tile = cross.shape[0] // 2
    row = lax.broadcasted_iota(jnp.int32, (tile, tile), 0)
    col = lax.broadcasted_iota(jnp.int32, (tile, tile), 1)
    second = cross[tile:, tile:]
    ends = jnp.where(row >= col, cross[:tile, :tile], second)
    side = cross[tile:, :tile]
    diag = jnp.broadcast_to(
        jnp.sum(jnp.where(row == col, second, 0.0), axis=0, keepdims=True), (SUB, tile)
    )
    kept_ref[:tile, :] = jnp.where(low == 0, ends, side)
    sent_ref[:tile, :] = jnp.where(low == 0, side, ends)
    kept_ref[tile:, :] = diag
    sent_ref[tile:, :] = diag


def over_lanes(value, col, tile):
    return jnp.broadcast_to(value[:, col:col + 1], (SUB, tile))


def over_rows(value, row, tile):
    return jnp.broadcast_to(value[row:row + 1, :], (SUB, tile))


def tree(terms):
    while len(terms) > 1:
        terms = [terms[q] + terms[q + 1] for q in range(0, len(terms), 2)]
    return terms[0]


def panel(blocks, group):
    count = len(blocks)
    blocks = list(blocks)
    tile = count * SUB
    lane = lax.broadcasted_iota(jnp.int32, (SUB, tile), 1)
    row = lax.broadcasted_iota(jnp.int32, (SUB, tile), 0)
    upper, inverse, pending = [], [], []
    for i in range(count):
        first = SUB * i
        own = blocks[i]
        end = min(count, (i // group + 1) * group)
        if i % group == 0:
            ahead = [over_lanes(own, first + k, tile) for k in range(SUB)]
        cols, e = ahead, {}
        inside = (lane >= first) & (lane < first + SUB)
        later = {
            t: [over_lanes(blocks[t], first + k, tile) for k in range(SUB)]
            for t in range(i + 1, end)
        }
        if i + 1 < end:
            ahead = [over_lanes(blocks[i + 1], first + SUB + k, tile) for k in range(SUB)]
        rows = [
            jnp.where(inside, jnp.where(lane == first + j, 1.0, 0.0), over_rows(own, j, tile))
            for j in range(SUB)
        ]
        for j in range(SUB):
            line = [over_rows(cols[k], j, tile) for k in range(j, SUB)]
            s = lax.rsqrt(line[0])
            for k in range(j, SUB):
                e[j, k] = line[k - j] * s
            down = cols[j] * s
            for k in range(j + 1, SUB):
                cols[k] = cols[k] - down * e[j, k]
            rows[j] = rows[j] * s
            for t in later:
                later[t][j] = later[t][j] * s
            for k in range(j + 1, SUB):
                rows[k] = rows[k] - e[j, k] * rows[j]
                for t in later:
                    later[t][k] = later[t][k] - e[j, k] * later[t][j]
        if i + 1 < end:
            nxt = later[i + 1]
            for k in range(SUB):
                ahead[k] = ahead[k] - tree([nxt[j] * over_rows(nxt[j], k, tile) for j in range(SUB)])
        for t in later:
            update = tree([later[t][j] * rows[j] for j in range(SUB)])
            blocks[t] = jnp.where(inside, 0.0, blocks[t]) - update
        up = jnp.zeros((SUB, tile), jnp.float32)
        full = up
        for j in range(SUB):
            line = jnp.where(lane >= first + SUB, rows[j], 0.0)
            for k in range(j, SUB):
                line = jnp.where(lane == first + k, e[j, k], line)
            up = jnp.where(row == j, line, up)
            full = jnp.where(row == j, rows[j], full)
        pending.append(jnp.where((lane >= first + SUB) & (lane < SUB * end), 0.0, full))
        upper.append(up)
        inverse.append(jnp.where(lane < first + SUB, full, 0.0))
        if i + 1 == end < count:
            done = jnp.concatenate(pending, 0)
            pending = []
            rest = SUB * end
            update = tn(done[:, rest:], done)
            here = (lane >= rest - group * SUB) & (lane < rest)
            for t in range(end, count):
                at = SUB * t - rest
                blocks[t] = jnp.where(here, 0.0, blocks[t]) - update[at:at + SUB, :]
    return jnp.concatenate(upper, 0), jnp.concatenate(inverse, 0)


def back_kernel(points_total, chunks, part_ref, other_ref, *refs):
    sketch_refs = refs[:chunks]
    basis_out, factor_out, basis_ref, factor_ref, sem = refs[chunks:]
    tile = part_ref.shape[1]
    low = lax.axis_index("pts") % 2
    part = part_ref[...] / points_total
    other = other_ref[...] / points_total
    ends = jnp.where(low == 0, part[:tile], other[:tile])
    side = jnp.where(low == 0, other[:tile], part[:tile])
    diag = jnp.where(low == 0, other[tile:tile + 1], part[tile:tile + 1])
    row = lax.broadcasted_iota(jnp.int32, (tile, tile), 0)
    col = lax.broadcasted_iota(jnp.int32, (tile, tile), 1)
    ends_t = ends.T
    side_t = side.T
    split = lambda a: [a[SUB * t:SUB * (t + 1), :] for t in range(tile // SUB)]
    group = max(1, tile // SUB // 2)
    copies = []

    def put(src, dst):
        copies.append(pltpu.make_async_copy(src, dst, sem.at[len(copies)]))
        copies[-1].start()

    up, inv1 = panel(split(jnp.where(row >= col, ends, ends_t)), group)
    factor_ref[:tile, :tile] = up
    factor_ref[tile:, :tile] = jnp.zeros((tile, tile), jnp.float32)
    right = nn(inv1, side_t)
    right_t = nt(side, inv1)
    factor_ref[:tile, tile:] = right
    rest = jnp.where(row < col, ends, jnp.where(row == col, diag, ends_t)) - nn(right_t, right)
    middle, at = [], 0
    for ref in sketch_refs:
        size = ref.shape[0]
        left = nt(ref[:, :tile], inv1)
        basis_ref[at:at + size, :tile] = left
        middle.append(ref[:, tile:] - nn(left, right))
        at += size
    put(factor_ref.at[:tile, :], factor_out.at[:tile, :])
    put(basis_ref.at[:, :tile], basis_out.at[:, :tile])
    up, inv2 = panel(split(rest), group)
    factor_ref[tile:, tile:] = up
    put(factor_ref.at[tile:, :], factor_out.at[tile:, :])
    at = 0
    for value in middle:
        size = value.shape[0]
        basis_ref[at:at + size, tile:] = nt(value, inv2)
        put(basis_ref.at[at:at + size, tile:], basis_out.at[at:at + size, tile:])
        at += size
    for copy in copies:
        copy.wait()


def chunk_widths(own_rows):
    step = own_rows // 4
    if step % 128:
        return [own_rows]
    return [step] * 4


def on_device(precip, thresholds, bin_index, test_matrix):
    tm_count = lax.axis_size("tm")
    pts_count = lax.axis_size("pts")
    days_local, points_local = precip.shape
    columns = test_matrix.shape[1]
    tile = columns // 2
    own_rows = points_local // tm_count
    days_total = days_local * tm_count
    points_total = points_local * pts_count
    f32 = jnp.float32

    rows = harmonic_filter(days_total)
    filt = rows.reshape(rows.shape[0], tm_count, days_local).transpose(1, 0, 2)
    filt = jnp.asarray(filt)
    thr = thresholds[:, None]
    bins = bin_index[None, :]

    vmem = pl.BlockSpec(memory_space=pltpu.VMEM)
    widths = chunk_widths(own_rows)
    size = days_local // len(QUARTERS)
    mine = lax.dynamic_slice_in_dim(
        test_matrix, (lax.axis_index("pts") % len(QUARTERS)) * size, size, 0
    )
    shapes = [
        jax.ShapeDtypeStruct((days_local, width), f32)
        for width in widths
        for _ in range(tm_count - 1)
    ]
    pieces = pl.pallas_call(
        functools.partial(cut_kernel, widths, own_rows, tm_count),
        out_shape=shapes,
        in_specs=[pl.BlockSpec(memory_space=pl.ANY)],
        out_specs=[vmem] * len(shapes),
        scratch_shapes=[pltpu.SemaphoreType.DMA((len(shapes),))],
        compiler_params=pltpu.CompilerParams(vmem_limit_bytes=4 << 20),
        name="cut",
    )(precip)
    sends = [("rows", mine, k) for k in range(1, tm_count)]
    for n in range(len(widths)):
        sends += [("points", pieces[n * (tm_count - 1) + k - 1], k) for k in range(1, tm_count)]
    came = []
    for _, value, k in sends:
        came.append(swap(value, k * pts_count))
    quarters, came = came[:tm_count - 1], came[tm_count - 1:]
    received = [came[n * (tm_count - 1):(n + 1) * (tm_count - 1)] for n in range(len(widths))]
    spread = []
    for got in quarters:
        beside = swap(got, 2)
        spread += [got, swap(got, 1)]
        spread += [beside, swap(beside, 1)]

    sketches, waiting = [], []
    cross = None
    start = 0
    for index, width in enumerate(widths):
        last = index == len(widths) - 1
        with_cross = last or sum(v.shape[0] for v in waiting) + width >= columns
        if sketches:
            received[index], sketches[-1] = lax.optimization_barrier((received[index], sketches[-1]))
        operands = [precip, thr, bins, filt, test_matrix] + received[index] + spread
        operands += waiting if with_cross else []
        operands += [cross] if with_cross and cross is not None else []
        shapes = [jax.ShapeDtypeStruct((width, columns), f32)]
        if last:
            shapes += [jax.ShapeDtypeStruct((tile + SUB, tile), f32)] * 2
        elif with_cross:
            shapes += [jax.ShapeDtypeStruct((columns, columns), f32)]
        out = pl.pallas_call(
            functools.partial(
                front_kernel,
                start,
                width,
                own_rows,
                tm_count,
                len(waiting) if with_cross else 0,
                with_cross and cross is not None,
                with_cross,
                last,
            ),
            out_shape=shapes,
            in_specs=[vmem] * len(operands),
            out_specs=[vmem] * len(shapes),
            scratch_shapes=[pltpu.VMEM((days_total, columns), f32)],
            cost_estimate=pl.CostEstimate(
                flops=12 * width * columns * (days_total + columns),
                bytes_accessed=4 * days_total * (width + columns),
                transcendentals=0,
            ),
            compiler_params=pltpu.CompilerParams(vmem_limit_bytes=16 << 20),
        )(*operands)
        sketches.append(out[0])
        if with_cross:
            waiting = []
            cross = out[1]
        else:
            waiting.append(out[0])
        start += width
    kept, sent = out[1], out[2]

    part = kept + swap(sent, 1)
    bits = [1 << n for n in range(1, (tm_count * pts_count).bit_length() - 1)]
    groups = []
    while bits:
        ends = {bits.pop(0), bits.pop() if bits else 0}
        groups.append(tuple(sorted(ends)) if len(ends) == 2 and 0 not in ends else (max(ends),))
    for even, odd in zip(groups, partners_order(groups)):
        steps = list(zip(partners(even), partners(odd)))
        got = [swap(part, *pair) for pair in steps]
        while len(got) > 1:
            got = [sum(got[n:n + 2][1:], got[n]) for n in range(0, len(got), 2)]
        part = part + got[0]
    other = swap(part, 1)

    basis, factor = pl.pallas_call(
        functools.partial(back_kernel, points_total, len(sketches)),
        out_shape=(
            jax.ShapeDtypeStruct((own_rows, columns), f32),
            jax.ShapeDtypeStruct((columns, columns), f32),
        ),
        in_specs=[vmem] * (2 + len(sketches)),
        out_specs=(pl.BlockSpec(memory_space=pltpu.HBM),) * 2,
        scratch_shapes=[
            pltpu.VMEM((own_rows, columns), f32),
            pltpu.VMEM((columns, columns), f32),
            pltpu.SemaphoreType.DMA((3 + len(sketches),)),
        ],
        compiler_params=pltpu.CompilerParams(vmem_limit_bytes=16 << 20),
        name="back",
    )(part, other, *sketches)
    return basis, factor


def solution(mesh):
    in_specs = (P("tm", "pts"), P(), P("pts"), P("tm", None))
    out_specs = (P(("pts", "tm"), None), P())

    return jax.shard_map(
        on_device, mesh=mesh, in_specs=in_specs, out_specs=out_specs, check_vma=False
    )
```

```python
import functools
import math

import jax
import jax.numpy as jnp
import numpy as np
from jax import lax
from jax.experimental import pallas as pl
from jax.experimental.pallas import tpu as pltpu
from jax.sharding import PartitionSpec as P


HARM = 8
SUB = 8
AXES = ("tm", "pts")
QUARTERS = (0, 1, 2, 3)
HI = lax.Precision.HIGHEST

year_days = 365.25


def harmonic_filter(days_total):
    phase_base = np.arange(days_total).astype(np.float32)
    columns = [np.ones_like(phase_base)]
    for order in range(1, HARM + 1):
        phase = np.float32(2.0 * math.pi * order / year_days) * phase_base
        columns.append(np.cos(phase.astype(np.float64)))
        columns.append(np.sin(phase.astype(np.float64)))
    table = np.stack(columns, 0).astype(np.float32).astype(np.float64)
    low = np.linalg.cholesky(table @ table.T)
    rows = np.linalg.solve(low, table)
    padded = -(-rows.shape[0] // SUB) * SUB
    rows = np.concatenate([rows, np.zeros((padded - rows.shape[0], days_total))], 0)
    return rows.astype(np.float32)


def nn(a, b):
    return jnp.dot(a, b, precision=HI, preferred_element_type=jnp.float32)


def nt(a, b):
    return lax.dot_general(
        a, b, (((1,), (1,)), ((), ())), precision=HI, preferred_element_type=jnp.float32
    )


def tn(a, b):
    return lax.dot_general(
        a, b, (((0,), (0,)), ((), ())), precision=HI, preferred_element_type=jnp.float32
    )


def swap(value, bit, odd_bit=None):
    total = lax.axis_size("tm") * lax.axis_size("pts")
    odd_bit = bit if odd_bit is None else odd_bit
    return lax.ppermute(
        value, AXES, [(i, i ^ (odd_bit if i % 2 else bit)) for i in range(total)]
    )


def partners(bits):
    return list(bits) + ([bits[0] ^ bits[1]] if len(bits) == 2 else [])


def partners_order(groups):
    return groups[::-1] if len({len(g) for g in groups}) == 1 else groups


def cut_kernel(widths, own_rows, tm_count, days_ref, *refs):
    piece_refs, sem = refs[:-1], refs[-1]
    place = lax.axis_index("tm")
    copies = []
    start = 0
    for width in widths:
        for k in range(1, tm_count):
            at = pl.multiple_of((place ^ k) * own_rows + start, math.gcd(own_rows, start))
            n = len(copies)
            copies.append(
                pltpu.make_async_copy(days_ref.at[:, pl.ds(at, width)], piece_refs[n], sem.at[n])
            )
        start += width
    for copy in copies:
        copy.start()
    for copy in copies:
        copy.wait()


def hold_kernel(test_ref, held_ref):
    held_ref[...] = test_ref[...]


def front_kernel(start, width, own_rows, tm_count, earlier, with_acc, with_cross, last, *refs):
    refs = list(refs)
    take = lambda n: [refs.pop(0) for _ in range(n)]
    days_ref, thr_ref, bin_ref, filt_ref, test_ref = take(5)
    recv_refs = take(tm_count - 1)
    quarter_refs = take(len(QUARTERS) * (tm_count - 1))
    earlier_refs = take(earlier)
    acc_refs = take(1 if with_acc else 0)
    sketch_ref = take(1)[0]
    outs = take(2 if last else int(with_cross))
    table_ref = take(1)[0]
    days_local = days_ref.shape[0]
    place = lax.axis_index("tm")
    pts_place = lax.axis_index("pts")
    low = pts_place % 2
    at = pl.multiple_of(place * own_rows + start, math.gcd(own_rows, start))
    table_ref[:days_local, :] = test_ref[...]
    size = days_local // len(QUARTERS)
    for n, ref in enumerate(quarter_refs):
        peer, q = divmod(n, len(QUARTERS))
        base = days_local * (peer + 1) + ((pts_place % len(QUARTERS)) ^ QUARTERS[q]) * size
        table_ref[pl.ds(pl.multiple_of(base, size), size), :] = ref[...]
    bins = bin_ref[:, pl.ds(at, width)]
    count = thr_ref.shape[0]
    entry = lax.broadcasted_iota(jnp.int32, (count, width), 0)
    level = jnp.sum(jnp.where(entry == bins, thr_ref[...], 0.0), axis=0, keepdims=True)
    series = [days_ref[:, pl.ds(at, width)]] + [r[...] for r in recv_refs]
    proj = nn(filt_ref[place], series[0])
    for k in range(1, tm_count):
        proj = proj + nn(filt_ref[place ^ k], series[k])
    excess = [
        jnp.maximum(series[k] - tn(filt_ref[place ^ k], proj) - level, 0.0)
        for k in range(tm_count)
    ]
    sketch = tn(jnp.concatenate(excess, 0), table_ref[...])
    sketch_ref[...] = sketch
    if not with_cross:
        return
    whole = jnp.concatenate([r[...] for r in earlier_refs] + [sketch], 0)
    cross = tn(whole, whole)
    for ref in acc_refs:
        cross = cross + ref[...]
    if not last:
        outs[0][...] = cross
        return
    kept_ref, sent_ref = outs
    tile = cross.shape[0] // 2
    row = lax.broadcasted_iota(jnp.int32, (tile, tile), 0)
    col = lax.broadcasted_iota(jnp.int32, (tile, tile), 1)
    second = cross[tile:, tile:]
    ends = jnp.where(row >= col, cross[:tile, :tile], second)
    side = cross[tile:, :tile]
    diag = jnp.broadcast_to(
        jnp.sum(jnp.where(row == col, second, 0.0), axis=0, keepdims=True), (SUB, tile)
    )
    kept_ref[:tile, :] = jnp.where(low == 0, ends, side)
    sent_ref[:tile, :] = jnp.where(low == 0, side, ends)
    kept_ref[tile:, :] = diag
    sent_ref[tile:, :] = diag


def over_lanes(value, col, tile):
    return jnp.broadcast_to(value[:, col:col + 1], (SUB, tile))


def over_rows(value, row, tile):
    return jnp.broadcast_to(value[row:row + 1, :], (SUB, tile))


def tree(terms):
    while len(terms) > 1:
        terms = [terms[q] + terms[q + 1] for q in range(0, len(terms), 2)]
    return terms[0]


def panel(blocks, group):
    count = len(blocks)
    blocks = list(blocks)
    tile = count * SUB
    lane = lax.broadcasted_iota(jnp.int32, (SUB, tile), 1)
    row = lax.broadcasted_iota(jnp.int32, (SUB, tile), 0)
    upper, inverse, pending = [], [], []
    for i in range(count):
        first = SUB * i
        own = blocks[i]
        end = min(count, (i // group + 1) * group)
        if i % group == 0:
            ahead = [over_lanes(own, first + k, tile) for k in range(SUB)]
        cols, e = ahead, {}
        inside = (lane >= first) & (lane < first + SUB)
        later = {
            t: [over_lanes(blocks[t], first + k, tile) for k in range(SUB)]
            for t in range(i + 1, end)
        }
        if i + 1 < end:
            ahead = [over_lanes(blocks[i + 1], first + SUB + k, tile) for k in range(SUB)]
        rows = [
            jnp.where(inside, jnp.where(lane == first + j, 1.0, 0.0), over_rows(own, j, tile))
            for j in range(SUB)
        ]
        for j in range(SUB):
            line = [over_rows(cols[k], j, tile) for k in range(j, SUB)]
            s = lax.rsqrt(line[0])
            for k in range(j, SUB):
                e[j, k] = line[k - j] * s
            down = cols[j] * s
            for k in range(j + 1, SUB):
                cols[k] = cols[k] - down * e[j, k]
            rows[j] = rows[j] * s
            for t in later:
                later[t][j] = later[t][j] * s
            for k in range(j + 1, SUB):
                rows[k] = rows[k] - e[j, k] * rows[j]
                for t in later:
                    later[t][k] = later[t][k] - e[j, k] * later[t][j]
        if i + 1 < end:
            nxt = later[i + 1]
            for k in range(SUB):
                ahead[k] = ahead[k] - tree([nxt[j] * over_rows(nxt[j], k, tile) for j in range(SUB)])
        for t in later:
            update = tree([later[t][j] * rows[j] for j in range(SUB)])
            blocks[t] = jnp.where(inside, 0.0, blocks[t]) - update
        up = jnp.zeros((SUB, tile), jnp.float32)
        full = up
        for j in range(SUB):
            line = jnp.where(lane >= first + SUB, rows[j], 0.0)
            for k in range(j, SUB):
                line = jnp.where(lane == first + k, e[j, k], line)
            up = jnp.where(row == j, line, up)
            full = jnp.where(row == j, rows[j], full)
        pending.append(jnp.where((lane >= first + SUB) & (lane < SUB * end), 0.0, full))
        upper.append(up)
        inverse.append(jnp.where(lane < first + SUB, full, 0.0))
        if i + 1 == end < count:
            done = jnp.concatenate(pending, 0)
            pending = []
            rest = SUB * end
            update = tn(done[:, rest:], done)
            here = (lane >= rest - group * SUB) & (lane < rest)
            for t in range(end, count):
                at = SUB * t - rest
                blocks[t] = jnp.where(here, 0.0, blocks[t]) - update[at:at + SUB, :]
    return jnp.concatenate(upper, 0), jnp.concatenate(inverse, 0)


def back_kernel(points_total, chunks, part_ref, other_ref, *refs):
    sketch_refs = refs[:chunks]
    basis_out, factor_out, basis_ref, factor_ref, sem = refs[chunks:]
    tile = part_ref.shape[1]
    low = lax.axis_index("pts") % 2
    part = part_ref[...] / points_total
    other = other_ref[...] / points_total
    ends = jnp.where(low == 0, part[:tile], other[:tile])
    side = jnp.where(low == 0, other[:tile], part[:tile])
    diag = jnp.where(low == 0, other[tile:tile + 1], part[tile:tile + 1])
    row = lax.broadcasted_iota(jnp.int32, (tile, tile), 0)
    col = lax.broadcasted_iota(jnp.int32, (tile, tile), 1)
    ends_t = ends.T
    side_t = side.T
    split = lambda a: [a[SUB * t:SUB * (t + 1), :] for t in range(tile // SUB)]
    group = max(1, tile // SUB // 2)
    copies = []

    def put(src, dst):
        copies.append(pltpu.make_async_copy(src, dst, sem.at[len(copies)]))
        copies[-1].start()

    up, inv1 = panel(split(jnp.where(row >= col, ends, ends_t)), group)
    factor_ref[:tile, :tile] = up
    factor_ref[tile:, :tile] = jnp.zeros((tile, tile), jnp.float32)
    right = nn(inv1, side_t)
    right_t = nt(side, inv1)
    factor_ref[:tile, tile:] = right
    rest = jnp.where(row < col, ends, jnp.where(row == col, diag, ends_t)) - nn(right_t, right)
    middle, at = [], 0
    for ref in sketch_refs:
        size = ref.shape[0]
        left = nt(ref[:, :tile], inv1)
        basis_ref[at:at + size, :tile] = left
        middle.append(ref[:, tile:] - nn(left, right))
        at += size
    put(factor_ref.at[:tile, :], factor_out.at[:tile, :])
    put(basis_ref.at[:, :tile], basis_out.at[:, :tile])
    up, inv2 = panel(split(rest), group)
    factor_ref[tile:, tile:] = up
    put(factor_ref.at[tile:, :], factor_out.at[tile:, :])
    at = 0
    for value in middle:
        size = value.shape[0]
        basis_ref[at:at + size, tile:] = nt(value, inv2)
        put(basis_ref.at[at:at + size, tile:], basis_out.at[at:at + size, tile:])
        at += size
    for copy in copies:
        copy.wait()


def chunk_widths(own_rows):
    step = own_rows // 4
    if step % 128:
        return [own_rows]
    return [step] * 4


def on_device(precip, thresholds, bin_index, test_matrix):
    tm_count = lax.axis_size("tm")
    pts_count = lax.axis_size("pts")
    days_local, points_local = precip.shape
    columns = test_matrix.shape[1]
    tile = columns // 2
    own_rows = points_local // tm_count
    days_total = days_local * tm_count
    points_total = points_local * pts_count
    f32 = jnp.float32

    rows = harmonic_filter(days_total)
    filt = rows.reshape(rows.shape[0], tm_count, days_local).transpose(1, 0, 2)
    filt = jnp.asarray(filt)
    thr = thresholds[:, None]
    bins = bin_index[None, :]

    vmem = pl.BlockSpec(memory_space=pltpu.VMEM)
    widths = chunk_widths(own_rows)
    size = days_local // len(QUARTERS)
    mine = lax.dynamic_slice_in_dim(
        test_matrix, (lax.axis_index("pts") % len(QUARTERS)) * size, size, 0
    )
    shapes = [
        jax.ShapeDtypeStruct((days_local, width), f32)
        for width in widths
        for _ in range(tm_count - 1)
    ]
    pieces = pl.pallas_call(
        functools.partial(cut_kernel, widths, own_rows, tm_count),
        out_shape=shapes,
        in_specs=[pl.BlockSpec(memory_space=pl.ANY)],
        out_specs=[vmem] * len(shapes),
        scratch_shapes=[pltpu.SemaphoreType.DMA((len(shapes),))],
        compiler_params=pltpu.CompilerParams(vmem_limit_bytes=4 << 20),
        name="cut",
    )(precip)
    held = pl.pallas_call(
        hold_kernel,
        out_shape=jax.ShapeDtypeStruct(test_matrix.shape, f32),
        in_specs=[vmem],
        out_specs=vmem,
        compiler_params=pltpu.CompilerParams(vmem_limit_bytes=4 << 20),
        name="hold",
    )(test_matrix)
    sends = [("rows", mine, k) for k in range(1, tm_count)]
    for n in range(len(widths)):
        sends += [("points", pieces[n * (tm_count - 1) + k - 1], k) for k in range(1, tm_count)]
    came = []
    for _, value, k in sends:
        came.append(swap(value, k * pts_count))
    quarters, came = came[:tm_count - 1], came[tm_count - 1:]
    received = [came[n * (tm_count - 1):(n + 1) * (tm_count - 1)] for n in range(len(widths))]
    spread = []
    for got in quarters:
        beside = swap(got, 2)
        spread += [got, swap(got, 1)]
        spread += [beside, swap(beside, 1)]

    sketches, waiting = [], []
    cross = None
    start = 0
    for index, width in enumerate(widths):
        last = index == len(widths) - 1
        with_cross = last or sum(v.shape[0] for v in waiting) + width >= columns
        if sketches:
            received[index], sketches[-1] = lax.optimization_barrier((received[index], sketches[-1]))
        operands = [precip, thr, bins, filt, held] + received[index] + spread
        operands += waiting if with_cross else []
        operands += [cross] if with_cross and cross is not None else []
        shapes = [jax.ShapeDtypeStruct((width, columns), f32)]
        if last:
            shapes += [jax.ShapeDtypeStruct((tile + SUB, tile), f32)] * 2
        elif with_cross:
            shapes += [jax.ShapeDtypeStruct((columns, columns), f32)]
        out = pl.pallas_call(
            functools.partial(
                front_kernel,
                start,
                width,
                own_rows,
                tm_count,
                len(waiting) if with_cross else 0,
                with_cross and cross is not None,
                with_cross,
                last,
            ),
            out_shape=shapes,
            in_specs=[vmem] * len(operands),
            out_specs=[vmem] * len(shapes),
            scratch_shapes=[pltpu.VMEM((days_total, columns), f32)],
            cost_estimate=pl.CostEstimate(
                flops=12 * width * columns * (days_total + columns),
                bytes_accessed=4 * days_total * (width + columns),
                transcendentals=0,
            ),
            compiler_params=pltpu.CompilerParams(vmem_limit_bytes=16 << 20),
        )(*operands)
        sketches.append(out[0])
        if with_cross:
            waiting = []
            cross = out[1]
        else:
            waiting.append(out[0])
        start += width
    kept, sent = out[1], out[2]

    part = kept + swap(sent, 1)
    bits = [1 << n for n in range(1, (tm_count * pts_count).bit_length() - 1)]
    groups = []
    while bits:
        ends = {bits.pop(0), bits.pop() if bits else 0}
        groups.append(tuple(sorted(ends)) if len(ends) == 2 and 0 not in ends else (max(ends),))
    for even, odd in zip(groups, partners_order(groups)):
        steps = list(zip(partners(even), partners(odd)))
        got = [swap(part, *pair) for pair in steps]
        while len(got) > 1:
            got = [sum(got[n:n + 2][1:], got[n]) for n in range(0, len(got), 2)]
        part = part + got[0]
    other = swap(part, 1)

    basis, factor = pl.pallas_call(
        functools.partial(back_kernel, points_total, len(sketches)),
        out_shape=(
            jax.ShapeDtypeStruct((own_rows, columns), f32),
            jax.ShapeDtypeStruct((columns, columns), f32),
        ),
        in_specs=[vmem] * (2 + len(sketches)),
        out_specs=(pl.BlockSpec(memory_space=pltpu.HBM),) * 2,
        scratch_shapes=[
            pltpu.VMEM((own_rows, columns), f32),
            pltpu.VMEM((columns, columns), f32),
            pltpu.SemaphoreType.DMA((3 + len(sketches),)),
        ],
        compiler_params=pltpu.CompilerParams(vmem_limit_bytes=16 << 20),
        name="back",
    )(part, other, *sketches)
    return basis, factor


def solution(mesh):
    in_specs = (P("tm", "pts"), P(), P("pts"), P("tm", None))
    out_specs = (P(("pts", "tm"), None), P())

    return jax.shard_map(
        on_device, mesh=mesh, in_specs=in_specs, out_specs=out_specs, check_vma=False
    )
```

```python
import functools
import math

import jax
import jax.numpy as jnp
import numpy as np
from jax import lax
from jax.experimental import pallas as pl
from jax.experimental.pallas import tpu as pltpu
from jax.sharding import PartitionSpec as P


HARM = 8
SUB = 8
AXES = ("tm", "pts")
QUARTERS = (0, 1, 2, 3)
HI = lax.Precision.HIGHEST

year_days = 365.25


def harmonic_filter(days_total):
    phase_base = np.arange(days_total).astype(np.float32)
    columns = [np.ones_like(phase_base)]
    for order in range(1, HARM + 1):
        phase = np.float32(2.0 * math.pi * order / year_days) * phase_base
        columns.append(np.cos(phase.astype(np.float64)))
        columns.append(np.sin(phase.astype(np.float64)))
    table = np.stack(columns, 0).astype(np.float32).astype(np.float64)
    low = np.linalg.cholesky(table @ table.T)
    rows = np.linalg.solve(low, table)
    padded = -(-rows.shape[0] // SUB) * SUB
    rows = np.concatenate([rows, np.zeros((padded - rows.shape[0], days_total))], 0)
    return rows.astype(np.float32)


def nn(a, b):
    return jnp.dot(a, b, precision=HI, preferred_element_type=jnp.float32)


def nt(a, b):
    return lax.dot_general(
        a, b, (((1,), (1,)), ((), ())), precision=HI, preferred_element_type=jnp.float32
    )


def tn(a, b):
    return lax.dot_general(
        a, b, (((0,), (0,)), ((), ())), precision=HI, preferred_element_type=jnp.float32
    )


def swap(value, bit, odd_bit=None):
    total = lax.axis_size("tm") * lax.axis_size("pts")
    odd_bit = bit if odd_bit is None else odd_bit
    return lax.ppermute(
        value, AXES, [(i, i ^ (odd_bit if i % 2 else bit)) for i in range(total)]
    )


def partners(bits):
    return list(bits) + ([bits[0] ^ bits[1]] if len(bits) == 2 else [])


def partners_order(groups):
    return groups[::-1] if len({len(g) for g in groups}) == 1 else groups


def cut_kernel(widths, own_rows, tm_count, days_ref, *refs):
    piece_refs, sem = refs[:-1], refs[-1]
    place = lax.axis_index("tm")
    copies = []
    start = 0
    for width in widths:
        for k in range(1, tm_count):
            at = pl.multiple_of((place ^ k) * own_rows + start, math.gcd(own_rows, start))
            n = len(copies)
            copies.append(
                pltpu.make_async_copy(days_ref.at[:, pl.ds(at, width)], piece_refs[n], sem.at[n])
            )
        start += width
    for copy in copies:
        copy.start()
    for copy in copies:
        copy.wait()


def hold_kernel(test_ref, held_ref):
    held_ref[...] = test_ref[...]


def front_kernel(start, width, own_rows, tm_count, earlier, with_acc, with_cross, last, *refs):
    refs = list(refs)
    take = lambda n: [refs.pop(0) for _ in range(n)]
    days_ref, thr_ref, bin_ref, filt_ref, test_ref = take(5)
    recv_refs = take(tm_count - 1)
    quarter_refs = take(len(QUARTERS) * (tm_count - 1))
    earlier_refs = take(earlier)
    acc_refs = take(1 if with_acc else 0)
    sketch_ref = take(1)[0]
    outs = take(2 if last else int(with_cross))
    table_ref = take(1)[0]
    days_local = days_ref.shape[0]
    place = lax.axis_index("tm")
    pts_place = lax.axis_index("pts")
    low = pts_place % 2
    at = pl.multiple_of(place * own_rows + start, math.gcd(own_rows, start))
    table_ref[:days_local, :] = test_ref[...]
    size = days_local // len(QUARTERS)
    for n, ref in enumerate(quarter_refs):
        peer, q = divmod(n, len(QUARTERS))
        base = days_local * (peer + 1) + ((pts_place % len(QUARTERS)) ^ QUARTERS[q]) * size
        table_ref[pl.ds(pl.multiple_of(base, size), size), :] = -ref[...]
    bins = bin_ref[:, pl.ds(at, width)]
    count = thr_ref.shape[0]
    entry = lax.broadcasted_iota(jnp.int32, (count, width), 0)
    level = jnp.sum(jnp.where(entry == bins, thr_ref[...], 0.0), axis=0, keepdims=True)
    level = jnp.broadcast_to(level, (SUB, width)).T[:, :1]
    series = [days_ref[:, pl.ds(at, width)]] + [r[...] for r in recv_refs]
    proj = nn(filt_ref[place], series[0])
    for k in range(1, tm_count):
        proj = proj + nn(filt_ref[place ^ k], series[k])
    proj = proj.T
    excess = [
        jnp.maximum(series[k].T - nn(proj, filt_ref[place ^ k]) - level, 0.0)
        for k in range(tm_count)
    ]
    sketch = nn(excess[0], table_ref[:days_local, :])
    for k in range(1, tm_count):
        sketch = sketch - nn(excess[k], table_ref[k * days_local:(k + 1) * days_local, :])
    sketch_ref[...] = sketch
    if not with_cross:
        return
    whole = jnp.concatenate([r[...] for r in earlier_refs] + [sketch], 0)
    tile = whole.shape[1] // 2
    cross = tn(whole, whole)
    top, below = cross[:tile, :tile], cross[tile:, :]
    for ref in acc_refs:
        top = top + ref[:tile, :tile]
        below = below + ref[tile:, :]
    if not last:
        outs[0][:tile, :tile] = top
        outs[0][:tile, tile:] = jnp.zeros((tile, tile), jnp.float32)
        outs[0][tile:, :] = below
        return
    kept_ref, sent_ref = outs
    row = lax.broadcasted_iota(jnp.int32, (tile, tile), 0)
    col = lax.broadcasted_iota(jnp.int32, (tile, tile), 1)
    second = below[:, tile:]
    ends = jnp.where(row >= col, top, second)
    side = below[:, :tile]
    diag = jnp.broadcast_to(
        jnp.sum(jnp.where(row == col, second, 0.0), axis=0, keepdims=True), (SUB, tile)
    )
    kept_ref[:tile, :] = jnp.where(low == 0, ends, side)
    sent_ref[:tile, :] = jnp.where(low == 0, side, ends)
    kept_ref[tile:, :] = diag
    sent_ref[tile:, :] = diag


def over_lanes(value, col, tile):
    return jnp.broadcast_to(value[:, col:col + 1], (SUB, tile))


def over_rows(value, row, tile):
    return jnp.broadcast_to(value[row:row + 1, :], (SUB, tile))


def tree(terms):
    while len(terms) > 1:
        terms = [terms[q] + terms[q + 1] for q in range(0, len(terms), 2)]
    return terms[0]


def panel(blocks, group):
    count = len(blocks)
    blocks = list(blocks)
    tile = count * SUB
    lane = lax.broadcasted_iota(jnp.int32, (SUB, tile), 1)
    row = lax.broadcasted_iota(jnp.int32, (SUB, tile), 0)
    upper, inverse, pending, corners = [], [], [], []
    for i in range(count):
        first = SUB * i
        own = blocks[i]
        corner = jnp.zeros((SUB, tile), jnp.float32)
        end = min(count, (i // group + 1) * group)
        if i % group == 0:
            ahead = [over_lanes(own, first + k, tile) for k in range(SUB)]
        cols, e = ahead, {}
        inside = (lane >= first) & (lane < first + SUB)
        later = {
            t: [over_lanes(blocks[t], first + k, tile) for k in range(SUB)]
            for t in range(i + 1, end)
        }
        if i + 1 < end:
            ahead = [over_lanes(blocks[i + 1], first + SUB + k, tile) for k in range(SUB)]
        rows = [
            jnp.where(inside, jnp.where(lane == first + j, 1.0, 0.0), over_rows(own, j, tile))
            for j in range(SUB)
        ]
        for j in range(SUB):
            line = [over_rows(cols[k], j, tile) for k in range(j, SUB)]
            s = lax.rsqrt(line[0])
            for k in range(j + 1, SUB):
                e[j, k] = line[k - j] * s
            down = cols[j] * s
            corner = jnp.where(lane == first + j, down, corner)
            for k in range(j + 1, SUB):
                cols[k] = cols[k] - down * e[j, k]
            rows[j] = rows[j] * s
            for t in later:
                later[t][j] = later[t][j] * s
            for k in range(j + 1, SUB):
                rows[k] = rows[k] - e[j, k] * rows[j]
                for t in later:
                    later[t][k] = later[t][k] - e[j, k] * later[t][j]
        if i + 1 < end:
            nxt = later[i + 1]
            for k in range(SUB):
                ahead[k] = ahead[k] - tree([nxt[j] * over_rows(nxt[j], k, tile) for j in range(SUB)])
        for t in later:
            update = tree([later[t][j] * rows[j] for j in range(SUB)])
            blocks[t] = jnp.where(inside, 0.0, blocks[t]) - update
        full = rows[0]
        for j in range(1, SUB):
            full = jnp.where(row == j, rows[j], full)
        corners.append(corner)
        pending.append(jnp.where((lane >= first + SUB) & (lane < SUB * end), 0.0, full))
        upper.append(jnp.where(lane >= first + SUB, full, 0.0))
        inverse.append(jnp.where(lane < first + SUB, full, 0.0))
        if i + 1 == end < count:
            done = jnp.concatenate(pending, 0)
            pending = []
            rest = SUB * end
            update = tn(done[:, rest:], done)
            here = (lane >= rest - group * SUB) & (lane < rest)
            for t in range(end, count):
                at = SUB * t - rest
                blocks[t] = jnp.where(here, 0.0, blocks[t]) - update[at:at + SUB, :]
    across = lax.broadcasted_iota(jnp.int32, (tile, tile), 1)
    along = lax.broadcasted_iota(jnp.int32, (tile, tile), 0)
    corners = jnp.concatenate(corners, 0).T
    inner = (across >= along) & (across // SUB == along // SUB)
    upper = jnp.where(inner, corners, jnp.concatenate(upper, 0))
    return upper, jnp.concatenate(inverse, 0)


def back_kernel(points_total, chunks, part_ref, other_ref, *refs):
    sketch_refs = refs[:chunks]
    basis_out, factor_out, basis_ref, factor_ref, sem = refs[chunks:]
    tile = part_ref.shape[1]
    low = lax.axis_index("pts") % 2
    part = part_ref[...] / points_total
    other = other_ref[...] / points_total
    ends = jnp.where(low == 0, part[:tile], other[:tile])
    side = jnp.where(low == 0, other[:tile], part[:tile])
    diag = jnp.where(low == 0, other[tile:tile + 1], part[tile:tile + 1])
    row = lax.broadcasted_iota(jnp.int32, (tile, tile), 0)
    col = lax.broadcasted_iota(jnp.int32, (tile, tile), 1)
    ends_t = ends.T
    side_t = side.T
    split = lambda a: [a[SUB * t:SUB * (t + 1), :] for t in range(tile // SUB)]
    group = max(1, tile // SUB // 2)
    copies = []

    def put(src, dst):
        copies.append(pltpu.make_async_copy(src, dst, sem.at[len(copies)]))
        copies[-1].start()

    up, inv1 = panel(split(jnp.where(row >= col, ends, ends_t)), group)
    factor_ref[:tile, :tile] = up
    factor_ref[tile:, :tile] = jnp.zeros((tile, tile), jnp.float32)
    right = nn(inv1, side_t)
    right_t = nt(side, inv1)
    factor_ref[:tile, tile:] = right
    rest = jnp.where(row < col, ends, jnp.where(row == col, diag, ends_t)) - nn(right_t, right)
    middle, at = [], 0
    for ref in sketch_refs:
        size = ref.shape[0]
        left = nt(ref[:, :tile], inv1)
        basis_ref[at:at + size, :tile] = left
        middle.append(ref[:, tile:] - nn(left, right))
        at += size
    put(factor_ref.at[:tile, :], factor_out.at[:tile, :])
    put(basis_ref.at[:, :tile], basis_out.at[:, :tile])
    up, inv2 = panel(split(rest), group)
    factor_ref[tile:, tile:] = up
    put(factor_ref.at[tile:, :], factor_out.at[tile:, :])
    at = 0
    for value in middle:
        size = value.shape[0]
        basis_ref[at:at + size, tile:] = nt(value, inv2)
        put(basis_ref.at[at:at + size, tile:], basis_out.at[at:at + size, tile:])
        at += size
    for copy in copies:
        copy.wait()


def chunk_widths(own_rows):
    step = own_rows // 4
    if step % 128:
        return [own_rows]
    return [step] * 4


def on_device(precip, thresholds, bin_index, test_matrix):
    tm_count = lax.axis_size("tm")
    pts_count = lax.axis_size("pts")
    days_local, points_local = precip.shape
    columns = test_matrix.shape[1]
    tile = columns // 2
    own_rows = points_local // tm_count
    days_total = days_local * tm_count
    points_total = points_local * pts_count
    f32 = jnp.float32

    rows = harmonic_filter(days_total)
    filt = rows.reshape(rows.shape[0], tm_count, days_local).transpose(1, 0, 2)
    filt = jnp.asarray(filt)
    thr = thresholds[:, None]
    bins = bin_index[None, :]

    vmem = pl.BlockSpec(memory_space=pltpu.VMEM)
    widths = chunk_widths(own_rows)
    size = days_local // len(QUARTERS)
    mine = lax.dynamic_slice_in_dim(
        test_matrix, (lax.axis_index("pts") % len(QUARTERS)) * size, size, 0
    )
    shapes = [
        jax.ShapeDtypeStruct((days_local, width), f32)
        for width in widths
        for _ in range(tm_count - 1)
    ]
    pieces = pl.pallas_call(
        functools.partial(cut_kernel, widths, own_rows, tm_count),
        out_shape=shapes,
        in_specs=[pl.BlockSpec(memory_space=pl.ANY)],
        out_specs=[vmem] * len(shapes),
        scratch_shapes=[pltpu.SemaphoreType.DMA((len(shapes),))],
        compiler_params=pltpu.CompilerParams(vmem_limit_bytes=4 << 20),
        name="cut",
    )(precip)
    held = pl.pallas_call(
        hold_kernel,
        out_shape=jax.ShapeDtypeStruct(test_matrix.shape, f32),
        in_specs=[vmem],
        out_specs=vmem,
        compiler_params=pltpu.CompilerParams(vmem_limit_bytes=4 << 20),
        name="hold",
    )(test_matrix)
    sends = [("rows", mine, k) for k in range(1, tm_count)]
    for n in range(len(widths)):
        sends += [("points", pieces[n * (tm_count - 1) + k - 1], k) for k in range(1, tm_count)]
    came = []
    for _, value, k in sends:
        came.append(swap(value, k * pts_count))
    quarters, came = came[:tm_count - 1], came[tm_count - 1:]
    received = [came[n * (tm_count - 1):(n + 1) * (tm_count - 1)] for n in range(len(widths))]
    spread = []
    for got in quarters:
        beside = swap(got, 2)
        spread += [got, swap(got, 1)]
        spread += [beside, swap(beside, 1)]

    sketches, waiting = [], []
    cross = None
    start = 0
    for index, width in enumerate(widths):
        last = index == len(widths) - 1
        with_cross = last or sum(v.shape[0] for v in waiting) + width >= columns
        if sketches:
            received[index], sketches[-1] = lax.optimization_barrier((received[index], sketches[-1]))
        operands = [precip, thr, bins, filt, held] + received[index] + spread
        operands += waiting if with_cross else []
        operands += [cross] if with_cross and cross is not None else []
        shapes = [jax.ShapeDtypeStruct((width, columns), f32)]
        if last:
            shapes += [jax.ShapeDtypeStruct((tile + SUB, tile), f32)] * 2
        elif with_cross:
            shapes += [jax.ShapeDtypeStruct((columns, columns), f32)]
        out = pl.pallas_call(
            functools.partial(
                front_kernel,
                start,
                width,
                own_rows,
                tm_count,
                len(waiting) if with_cross else 0,
                with_cross and cross is not None,
                with_cross,
                last,
            ),
            out_shape=shapes,
            in_specs=[vmem] * len(operands),
            out_specs=[vmem] * len(shapes),
            scratch_shapes=[pltpu.VMEM((days_total, columns), f32)],
            cost_estimate=pl.CostEstimate(
                flops=12 * width * columns * (days_total + columns),
                bytes_accessed=4 * days_total * (width + columns),
                transcendentals=0,
            ),
            compiler_params=pltpu.CompilerParams(vmem_limit_bytes=16 << 20),
        )(*operands)
        sketches.append(out[0])
        if with_cross:
            waiting = []
            cross = out[1]
        else:
            waiting.append(out[0])
        start += width
    kept, sent = out[1], out[2]

    part = kept + swap(sent, 1)
    bits = [1 << n for n in range(1, (tm_count * pts_count).bit_length() - 1)]
    groups = []
    while bits:
        ends = {bits.pop(0), bits.pop() if bits else 0}
        groups.append(tuple(sorted(ends)) if len(ends) == 2 and 0 not in ends else (max(ends),))
    for even, odd in zip(groups, partners_order(groups)):
        steps = list(zip(partners(even), partners(odd)))
        got = [swap(part, *pair) for pair in steps]
        while len(got) > 1:
            got = [sum(got[n:n + 2][1:], got[n]) for n in range(0, len(got), 2)]
        part = part + got[0]
    other = swap(part, 1)

    basis, factor = pl.pallas_call(
        functools.partial(back_kernel, points_total, len(sketches)),
        out_shape=(
            jax.ShapeDtypeStruct((own_rows, columns), f32),
            jax.ShapeDtypeStruct((columns, columns), f32),
        ),
        in_specs=[vmem] * (2 + len(sketches)),
        out_specs=(pl.BlockSpec(memory_space=pltpu.HBM),) * 2,
        scratch_shapes=[
            pltpu.VMEM((own_rows, columns), f32),
            pltpu.VMEM((columns, columns), f32),
            pltpu.SemaphoreType.DMA((3 + len(sketches),)),
        ],
        compiler_params=pltpu.CompilerParams(vmem_limit_bytes=16 << 20),
        name="back",
    )(part, other, *sketches)
    return basis, factor


def solution(mesh):
    in_specs = (P("tm", "pts"), P(), P("pts"), P("tm", None))
    out_specs = (P(("pts", "tm"), None), P())

    return jax.shard_map(
        on_device, mesh=mesh, in_specs=in_specs, out_specs=out_specs, check_vma=False
    )
```

```python
import functools
import math

import jax
import jax.numpy as jnp
import numpy as np
from jax import lax
from jax.experimental import pallas as pl
from jax.experimental.pallas import tpu as pltpu
from jax.sharding import PartitionSpec as P


HARM = 8
SUB = 8
AXES = ("tm", "pts")
QUARTERS = (0, 1, 2, 3)
HI = lax.Precision.HIGHEST

year_days = 365.25


def harmonic_filter(days_total):
    phase_base = np.arange(days_total).astype(np.float32)
    columns = [np.ones_like(phase_base)]
    for order in range(1, HARM + 1):
        phase = np.float32(2.0 * math.pi * order / year_days) * phase_base
        columns.append(np.cos(phase.astype(np.float64)))
        columns.append(np.sin(phase.astype(np.float64)))
    table = np.stack(columns, 0).astype(np.float32).astype(np.float64)
    low = np.linalg.cholesky(table @ table.T)
    rows = np.linalg.solve(low, table)
    padded = -(-rows.shape[0] // SUB) * SUB
    rows = np.concatenate([rows, np.zeros((padded - rows.shape[0], days_total))], 0)
    return rows.astype(np.float32)


def nn(a, b):
    return jnp.dot(a, b, precision=HI, preferred_element_type=jnp.float32)


def nt(a, b):
    return lax.dot_general(
        a, b, (((1,), (1,)), ((), ())), precision=HI, preferred_element_type=jnp.float32
    )


def tn(a, b):
    return lax.dot_general(
        a, b, (((0,), (0,)), ((), ())), precision=HI, preferred_element_type=jnp.float32
    )


def swap(value, bit, odd_bit=None):
    total = lax.axis_size("tm") * lax.axis_size("pts")
    odd_bit = bit if odd_bit is None else odd_bit
    return lax.ppermute(
        value, AXES, [(i, i ^ (odd_bit if i % 2 else bit)) for i in range(total)]
    )


def partners(bits):
    return list(bits) + ([bits[0] ^ bits[1]] if len(bits) == 2 else [])


def partners_order(groups):
    return groups[::-1] if len({len(g) for g in groups}) == 1 else groups


def cut_kernel(widths, own_rows, tm_count, days_ref, *refs):
    piece_refs, sem = refs[:-1], refs[-1]
    place = lax.axis_index("tm")
    copies = []
    start = 0
    for width in widths:
        for k in range(1, tm_count):
            at = pl.multiple_of((place ^ k) * own_rows + start, math.gcd(own_rows, start))
            n = len(copies)
            copies.append(
                pltpu.make_async_copy(days_ref.at[:, pl.ds(at, width)], piece_refs[n], sem.at[n])
            )
        start += width
    for copy in copies:
        copy.start()
    for copy in copies:
        copy.wait()


def hold_kernel(test_ref, held_ref):
    held_ref[...] = test_ref[...]


def front_kernel(start, width, own_rows, tm_count, earlier, with_acc, with_cross, last, *refs):
    refs = list(refs)
    take = lambda n: [refs.pop(0) for _ in range(n)]
    days_ref, thr_ref, bin_ref, filt_ref, test_ref = take(5)
    recv_refs = take(tm_count - 1)
    quarter_refs = take(len(QUARTERS) * (tm_count - 1))
    earlier_refs = take(earlier)
    acc_refs = take(1 if with_acc else 0)
    sketch_ref = take(1)[0]
    outs = take(2 if last else int(with_cross))
    table_ref = take(1)[0]
    days_local = days_ref.shape[0]
    place = lax.axis_index("tm")
    pts_place = lax.axis_index("pts")
    low = pts_place % 2
    at = pl.multiple_of(place * own_rows + start, math.gcd(own_rows, start))
    table_ref[:days_local, :] = test_ref[...]
    size = days_local // len(QUARTERS)
    for n, ref in enumerate(quarter_refs):
        peer, q = divmod(n, len(QUARTERS))
        base = days_local * (peer + 1) + ((pts_place % len(QUARTERS)) ^ QUARTERS[q]) * size
        table_ref[pl.ds(pl.multiple_of(base, size), size), :] = -ref[...]
    bins = bin_ref[:, pl.ds(at, width)]
    count = thr_ref.shape[0]
    entry = lax.broadcasted_iota(jnp.int32, (count, width), 0)
    level = jnp.sum(jnp.where(entry == bins, thr_ref[...], 0.0), axis=0, keepdims=True)
    level = jnp.broadcast_to(level, (SUB, width)).T[:, :1]
    series = [days_ref[:, pl.ds(at, width)]] + [r[...] for r in recv_refs]
    proj = nn(filt_ref[place], series[0])
    for k in range(1, tm_count):
        proj = proj + nn(filt_ref[place ^ k], series[k])
    proj = proj.T
    excess = [
        jnp.maximum(series[k].T - nn(proj, filt_ref[place ^ k]) - level, 0.0)
        for k in range(tm_count)
    ]
    sketch = nn(excess[0], table_ref[:days_local, :])
    for k in range(1, tm_count):
        sketch = sketch - nn(excess[k], table_ref[k * days_local:(k + 1) * days_local, :])
    sketch_ref[...] = sketch
    if not with_cross:
        return
    whole = jnp.concatenate([r[...] for r in earlier_refs] + [sketch], 0)
    tile = whole.shape[1] // 2
    cross = tn(whole, whole)
    top, below = cross[:tile, :tile], cross[tile:, :]
    for ref in acc_refs:
        top = top + ref[:tile, :tile]
        below = below + ref[tile:, :]
    if not last:
        outs[0][:tile, :tile] = top
        outs[0][:tile, tile:] = jnp.zeros((tile, tile), jnp.float32)
        outs[0][tile:, :] = below
        return
    kept_ref, sent_ref = outs
    row = lax.broadcasted_iota(jnp.int32, (tile, tile), 0)
    col = lax.broadcasted_iota(jnp.int32, (tile, tile), 1)
    second = below[:, tile:]
    ends = jnp.where(row >= col, top, second)
    side = below[:, :tile]
    diag = jnp.broadcast_to(
        jnp.sum(jnp.where(row == col, second, 0.0), axis=0, keepdims=True), (SUB, tile)
    )
    kept_ref[:tile, :] = jnp.where(low == 0, ends, side)
    sent_ref[:tile, :] = jnp.where(low == 0, side, ends)
    kept_ref[tile:, :] = diag
    sent_ref[tile:, :] = diag


def over_lanes(value, col, tile):
    return jnp.broadcast_to(value[:, col:col + 1], (SUB, tile))


def over_rows(value, row, tile):
    return jnp.broadcast_to(value[row:row + 1, :], (SUB, tile))


def tree(terms):
    while len(terms) > 1:
        terms = [terms[q] + terms[q + 1] for q in range(0, len(terms), 2)]
    return terms[0]


def panel(blocks, group, hooks):
    count = len(blocks)
    blocks = list(blocks)
    tile = count * SUB
    lane = lax.broadcasted_iota(jnp.int32, (SUB, tile), 1)
    row = lax.broadcasted_iota(jnp.int32, (SUB, tile), 0)
    upper, inverse, pending, corners = [], [], [], []
    for i in range(count):
        first = SUB * i
        own = blocks[i]
        corner = jnp.zeros((SUB, tile), jnp.float32)
        end = min(count, (i // group + 1) * group)
        if i % group == 0:
            ahead = [over_lanes(own, first + k, tile) for k in range(SUB)]
        cols, e = ahead, {}
        inside = (lane >= first) & (lane < first + SUB)
        later = {
            t: [over_lanes(blocks[t], first + k, tile) for k in range(SUB)]
            for t in range(i + 1, end)
        }
        if i + 1 < end:
            ahead = [over_lanes(blocks[i + 1], first + SUB + k, tile) for k in range(SUB)]
        rows = [
            jnp.where(inside, jnp.where(lane == first + j, 1.0, 0.0), over_rows(own, j, tile))
            for j in range(SUB)
        ]
        for j in range(SUB):
            line = [over_rows(cols[k], j, tile) for k in range(j, SUB)]
            s = lax.rsqrt(line[0])
            for k in range(j + 1, SUB):
                e[j, k] = line[k - j] * s
            down = cols[j] * s
            corner = jnp.where(lane == first + j, down, corner)
            for k in range(j + 1, SUB):
                cols[k] = cols[k] - down * e[j, k]
            rows[j] = rows[j] * s
            for t in later:
                later[t][j] = later[t][j] * s
            for k in range(j + 1, SUB):
                rows[k] = rows[k] - e[j, k] * rows[j]
                for t in later:
                    later[t][k] = later[t][k] - e[j, k] * later[t][j]
        if i + 1 < end:
            nxt = later[i + 1]
            for k in range(SUB):
                ahead[k] = ahead[k] - tree([nxt[j] * over_rows(nxt[j], k, tile) for j in range(SUB)])
        for t in later:
            update = tree([later[t][j] * rows[j] for j in range(SUB)])
            blocks[t] = jnp.where(inside, 0.0, blocks[t]) - update
        full = rows[0]
        for j in range(1, SUB):
            full = jnp.where(row == j, rows[j], full)
        corners.append(corner)
        pending.append(jnp.where((lane >= first + SUB) & (lane < SUB * end), 0.0, full))
        upper.append(jnp.where(lane >= first + SUB, full, 0.0))
        inverse.append(jnp.where(lane < first + SUB, full, 0.0))
        if i + 1 == end < count:
            done = jnp.concatenate(pending, 0)
            pending = []
            rest = SUB * end
            update = tn(done[:, rest:], done)
            here = (lane >= rest - group * SUB) & (lane < rest)
            for t in range(end, count):
                at = SUB * t - rest
                blocks[t] = jnp.where(here, 0.0, blocks[t]) - update[at:at + SUB, :]
        if i in hooks:
            hooks[i](inverse)
    across = lax.broadcasted_iota(jnp.int32, (tile, tile), 1)
    along = lax.broadcasted_iota(jnp.int32, (tile, tile), 0)
    corners = jnp.concatenate(corners, 0).T
    inner = (across >= along) & (across // SUB == along // SUB)
    upper = jnp.where(inner, corners, jnp.concatenate(upper, 0))
    return upper, jnp.concatenate(inverse, 0)


def back_kernel(points_total, chunks, part_ref, other_ref, *refs):
    sketch_refs = refs[:chunks]
    basis_out, factor_out, basis_ref, factor_ref, sem = refs[chunks:]
    tile = part_ref.shape[1]
    low = lax.axis_index("pts") % 2
    part = part_ref[...] / points_total
    other = other_ref[...] / points_total
    ends = jnp.where(low == 0, part[:tile], other[:tile])
    side = jnp.where(low == 0, other[:tile], part[:tile])
    diag = jnp.where(low == 0, other[tile:tile + 1], part[tile:tile + 1])
    row = lax.broadcasted_iota(jnp.int32, (tile, tile), 0)
    col = lax.broadcasted_iota(jnp.int32, (tile, tile), 1)
    ends_t = ends.T
    side_t = side.T
    split = lambda a: [a[SUB * t:SUB * (t + 1), :] for t in range(tile // SUB)]
    group = max(1, tile // SUB // 2)
    copies = []

    def put(src, dst):
        copies.append(pltpu.make_async_copy(src, dst, sem.at[len(copies)]))
        copies[-1].start()

    right = []
    rest = [jnp.where(row < col, ends, jnp.where(row == col, diag, ends_t))]

    def reduce_rest(inverse):
        inverse = jnp.concatenate(inverse[len(right) * group:(len(right) + 1) * group], 0)
        right.append(nn(inverse, side_t))
        rest.append(rest[-1] - nn(nt(side, inverse), right[-1]))

    last = tile // SUB - 1
    hooks = {min(last, end + 1): reduce_rest for end in range(group - 1, last, group)}
    hooks[last] = reduce_rest
    up, inv1 = panel(split(jnp.where(row >= col, ends, ends_t)), group, hooks)
    right = jnp.concatenate(right, 0)
    middle = []

    def first_half(_):
        factor_ref[:tile, :tile] = up
        factor_ref[tile:, :tile] = jnp.zeros((tile, tile), jnp.float32)
        factor_ref[:tile, tile:] = right
        sketch = jnp.concatenate([ref[...] for ref in sketch_refs], 0)
        left = nt(sketch[:, :tile], inv1)
        basis_ref[:, :tile] = left
        middle.append(sketch[:, tile:] - nn(left, right))
        put(factor_ref.at[:tile, :], factor_out.at[:tile, :])
        put(basis_ref.at[:, :tile], basis_out.at[:, :tile])

    up2, inv2 = panel(split(rest[-1]), group, {min(last, 1): first_half})
    middle = middle[0]
    step = basis_ref.shape[0] // 2
    for at in (0, step):
        basis_ref[at:at + step, tile:] = nt(middle[at:at + step], inv2)
        put(basis_ref.at[at:at + step, tile:], basis_out.at[at:at + step, tile:])
    factor_ref[tile:, tile:] = up2
    put(factor_ref.at[tile:, :], factor_out.at[tile:, :])
    for copy in copies:
        copy.wait()


def chunk_widths(own_rows):
    step = own_rows // 4
    if step % 128:
        return [own_rows]
    return [step] * 4


def on_device(precip, thresholds, bin_index, test_matrix):
    tm_count = lax.axis_size("tm")
    pts_count = lax.axis_size("pts")
    days_local, points_local = precip.shape
    columns = test_matrix.shape[1]
    tile = columns // 2
    own_rows = points_local // tm_count
    days_total = days_local * tm_count
    points_total = points_local * pts_count
    f32 = jnp.float32

    rows = harmonic_filter(days_total)
    filt = rows.reshape(rows.shape[0], tm_count, days_local).transpose(1, 0, 2)
    filt = jnp.asarray(filt)
    thr = thresholds[:, None]
    bins = bin_index[None, :]

    vmem = pl.BlockSpec(memory_space=pltpu.VMEM)
    widths = chunk_widths(own_rows)
    size = days_local // len(QUARTERS)
    mine = lax.dynamic_slice_in_dim(
        test_matrix, (lax.axis_index("pts") % len(QUARTERS)) * size, size, 0
    )
    shapes = [
        jax.ShapeDtypeStruct((days_local, width), f32)
        for width in widths
        for _ in range(tm_count - 1)
    ]
    pieces = pl.pallas_call(
        functools.partial(cut_kernel, widths, own_rows, tm_count),
        out_shape=shapes,
        in_specs=[pl.BlockSpec(memory_space=pl.ANY)],
        out_specs=[vmem] * len(shapes),
        scratch_shapes=[pltpu.SemaphoreType.DMA((len(shapes),))],
        compiler_params=pltpu.CompilerParams(vmem_limit_bytes=4 << 20),
        name="cut",
    )(precip)
    held = pl.pallas_call(
        hold_kernel,
        out_shape=jax.ShapeDtypeStruct(test_matrix.shape, f32),
        in_specs=[vmem],
        out_specs=vmem,
        compiler_params=pltpu.CompilerParams(vmem_limit_bytes=4 << 20),
        name="hold",
    )(test_matrix)
    sends = [("rows", mine, k) for k in range(1, tm_count)]
    for n in range(len(widths)):
        sends += [("points", pieces[n * (tm_count - 1) + k - 1], k) for k in range(1, tm_count)]
    came = []
    for _, value, k in sends:
        came.append(swap(value, k * pts_count))
    quarters, came = came[:tm_count - 1], came[tm_count - 1:]
    received = [came[n * (tm_count - 1):(n + 1) * (tm_count - 1)] for n in range(len(widths))]
    spread = []
    for got in quarters:
        beside = swap(got, 2)
        spread += [got, swap(got, 1)]
        spread += [beside, swap(beside, 1)]

    sketches, waiting = [], []
    cross = None
    start = 0
    for index, width in enumerate(widths):
        last = index == len(widths) - 1
        with_cross = last or sum(v.shape[0] for v in waiting) + width >= columns
        if sketches:
            received[index], sketches[-1] = lax.optimization_barrier((received[index], sketches[-1]))
        operands = [precip, thr, bins, filt, held] + received[index] + spread
        operands += waiting if with_cross else []
        operands += [cross] if with_cross and cross is not None else []
        shapes = [jax.ShapeDtypeStruct((width, columns), f32)]
        if last:
            shapes += [jax.ShapeDtypeStruct((tile + SUB, tile), f32)] * 2
        elif with_cross:
            shapes += [jax.ShapeDtypeStruct((columns, columns), f32)]
        out = pl.pallas_call(
            functools.partial(
                front_kernel,
                start,
                width,
                own_rows,
                tm_count,
                len(waiting) if with_cross else 0,
                with_cross and cross is not None,
                with_cross,
                last,
            ),
            out_shape=shapes,
            in_specs=[vmem] * len(operands),
            out_specs=[vmem] * len(shapes),
            scratch_shapes=[pltpu.VMEM((days_total, columns), f32)],
            cost_estimate=pl.CostEstimate(
                flops=12 * width * columns * (days_total + columns),
                bytes_accessed=4 * days_total * (width + columns),
                transcendentals=0,
            ),
            compiler_params=pltpu.CompilerParams(vmem_limit_bytes=16 << 20),
        )(*operands)
        sketches.append(out[0])
        if with_cross:
            waiting = []
            cross = out[1]
        else:
            waiting.append(out[0])
        start += width
    kept, sent = out[1], out[2]

    part = kept + swap(sent, 1)
    bits = [1 << n for n in range(1, (tm_count * pts_count).bit_length() - 1)]
    groups = []
    while bits:
        ends = {bits.pop(0), bits.pop() if bits else 0}
        groups.append(tuple(sorted(ends)) if len(ends) == 2 and 0 not in ends else (max(ends),))
    for even, odd in zip(groups, partners_order(groups)):
        steps = list(zip(partners(even), partners(odd)))
        got = [swap(part, *pair) for pair in steps]
        while len(got) > 1:
            got = [sum(got[n:n + 2][1:], got[n]) for n in range(0, len(got), 2)]
        part = part + got[0]
    other = swap(part, 1)

    basis, factor = pl.pallas_call(
        functools.partial(back_kernel, points_total, len(sketches)),
        out_shape=(
            jax.ShapeDtypeStruct((own_rows, columns), f32),
            jax.ShapeDtypeStruct((columns, columns), f32),
        ),
        in_specs=[vmem] * (2 + len(sketches)),
        out_specs=(pl.BlockSpec(memory_space=pltpu.HBM),) * 2,
        scratch_shapes=[
            pltpu.VMEM((own_rows, columns), f32),
            pltpu.VMEM((columns, columns), f32),
            pltpu.SemaphoreType.DMA((5,)),
        ],
        compiler_params=pltpu.CompilerParams(vmem_limit_bytes=16 << 20),
        name="back",
    )(part, other, *sketches)
    return basis, factor


def solution(mesh):
    in_specs = (P("tm", "pts"), P(), P("pts"), P("tm", None))
    out_specs = (P(("pts", "tm"), None), P())

    return jax.shard_map(
        on_device, mesh=mesh, in_specs=in_specs, out_specs=out_specs, check_vma=False
    )
```

```python
import functools
import math

import jax
import jax.numpy as jnp
import numpy as np
from jax import lax
from jax.experimental import pallas as pl
from jax.experimental.pallas import tpu as pltpu
from jax.sharding import PartitionSpec as P


HARM = 8
SUB = 8
AXES = ("tm", "pts")
QUARTERS = (0, 1, 2, 3)
HI = lax.Precision.HIGHEST

year_days = 365.25


def harmonic_filter(days_total):
    phase_base = np.arange(days_total).astype(np.float32)
    columns = [np.ones_like(phase_base)]
    for order in range(1, HARM + 1):
        phase = np.float32(2.0 * math.pi * order / year_days) * phase_base
        columns.append(np.cos(phase.astype(np.float64)))
        columns.append(np.sin(phase.astype(np.float64)))
    table = np.stack(columns, 0).astype(np.float32).astype(np.float64)
    low = np.linalg.cholesky(table @ table.T)
    rows = np.linalg.solve(low, table)
    padded = -(-rows.shape[0] // SUB) * SUB
    rows = np.concatenate([rows, np.zeros((padded - rows.shape[0], days_total))], 0)
    return rows.astype(np.float32)


def nn(a, b):
    return jnp.dot(a, b, precision=HI, preferred_element_type=jnp.float32)


def nt(a, b):
    return lax.dot_general(
        a, b, (((1,), (1,)), ((), ())), precision=HI, preferred_element_type=jnp.float32
    )


def tn(a, b):
    return lax.dot_general(
        a, b, (((0,), (0,)), ((), ())), precision=HI, preferred_element_type=jnp.float32
    )


def swap(value, bit, odd_bit=None):
    total = lax.axis_size("tm") * lax.axis_size("pts")
    odd_bit = bit if odd_bit is None else odd_bit
    return lax.ppermute(
        value, AXES, [(i, i ^ (odd_bit if i % 2 else bit)) for i in range(total)]
    )


def partners(bits):
    return list(bits) + ([bits[0] ^ bits[1]] if len(bits) == 2 else [])


def partners_order(groups):
    return groups[::-1] if len({len(g) for g in groups}) == 1 else groups


def cut_kernel(widths, own_rows, tm_count, days_ref, *refs):
    piece_refs, sem = refs[:-1], refs[-1]
    place = lax.axis_index("tm")
    copies = []
    start = 0
    for width in widths:
        for k in range(1, tm_count):
            at = pl.multiple_of((place ^ k) * own_rows + start, math.gcd(own_rows, start))
            n = len(copies)
            copies.append(
                pltpu.make_async_copy(days_ref.at[:, pl.ds(at, width)], piece_refs[n], sem.at[n])
            )
        start += width
    for copy in copies:
        copy.start()
    for copy in copies:
        copy.wait()


def hold_kernel(test_ref, held_ref):
    held_ref[...] = test_ref[...]


def front_kernel(start, width, own_rows, tm_count, earlier, with_acc, with_cross, last, *refs):
    refs = list(refs)
    take = lambda n: [refs.pop(0) for _ in range(n)]
    days_ref, thr_ref, bin_ref, filt_ref, test_ref = take(5)
    recv_refs = take(tm_count - 1)
    quarter_refs = take(len(QUARTERS) * (tm_count - 1))
    earlier_refs = take(earlier)
    acc_refs = take(1 if with_acc else 0)
    sketch_ref = take(1)[0]
    outs = take(2 if last else int(with_cross))
    table_ref = take(1)[0]
    days_local = days_ref.shape[0]
    place = lax.axis_index("tm")
    pts_place = lax.axis_index("pts")
    low = pts_place % 2
    at = pl.multiple_of(place * own_rows + start, math.gcd(own_rows, start))
    table_ref[:days_local, :] = test_ref[...]
    size = days_local // len(QUARTERS)
    for n, ref in enumerate(quarter_refs):
        peer, q = divmod(n, len(QUARTERS))
        base = days_local * (peer + 1) + ((pts_place % len(QUARTERS)) ^ QUARTERS[q]) * size
        table_ref[pl.ds(pl.multiple_of(base, size), size), :] = -ref[...]
    bins = bin_ref[:, pl.ds(at, width)]
    count = thr_ref.shape[0]
    entry = lax.broadcasted_iota(jnp.int32, (count, width), 0)
    level = jnp.sum(jnp.where(entry == bins, thr_ref[...], 0.0), axis=0, keepdims=True)
    level = jnp.broadcast_to(level, (SUB, width)).T[:, :1]
    series = [days_ref[:, pl.ds(at, width)]] + [r[...] for r in recv_refs]
    proj = nn(filt_ref[place], series[0])
    for k in range(1, tm_count):
        proj = proj + nn(filt_ref[place ^ k], series[k])
    proj = proj.T
    excess = [
        jnp.maximum(series[k].T - nn(proj, filt_ref[place ^ k]) - level, 0.0)
        for k in range(tm_count)
    ]
    sketch = nn(excess[0], table_ref[:days_local, :])
    for k in range(1, tm_count):
        sketch = sketch - nn(excess[k], table_ref[k * days_local:(k + 1) * days_local, :])
    sketch_ref[...] = sketch
    if not with_cross:
        return
    whole = jnp.concatenate([r[...] for r in earlier_refs] + [sketch], 0)
    tile = whole.shape[1] // 2
    cross = tn(whole, whole)
    top, below = cross[:tile, :tile], cross[tile:, :]
    for ref in acc_refs:
        top = top + ref[:tile, :tile]
        below = below + ref[tile:, :]
    if not last:
        outs[0][:tile, :tile] = top
        outs[0][:tile, tile:] = jnp.zeros((tile, tile), jnp.float32)
        outs[0][tile:, :] = below
        return
    kept_ref, sent_ref = outs
    row = lax.broadcasted_iota(jnp.int32, (tile, tile), 0)
    col = lax.broadcasted_iota(jnp.int32, (tile, tile), 1)
    second = below[:, tile:]
    ends = jnp.where(row >= col, top, second)
    side = below[:, :tile]
    diag = jnp.broadcast_to(
        jnp.sum(jnp.where(row == col, second, 0.0), axis=0, keepdims=True), (SUB, tile)
    )
    kept_ref[:tile, :] = jnp.where(low == 0, ends, side)
    sent_ref[:tile, :] = jnp.where(low == 0, side, ends)
    kept_ref[tile:, :] = diag
    sent_ref[tile:, :] = diag


def over_lanes(value, col, tile):
    return jnp.broadcast_to(value[:, col:col + 1], (SUB, tile))


def over_rows(value, row, tile):
    return jnp.broadcast_to(value[row:row + 1, :], (SUB, tile))


def tree(terms):
    while len(terms) > 1:
        terms = [terms[q] + terms[q + 1] for q in range(0, len(terms), 2)]
    return terms[0]


def panel(blocks, group, hooks):
    count = len(blocks)
    blocks = list(blocks)
    tile = count * SUB
    lane = lax.broadcasted_iota(jnp.int32, (SUB, tile), 1)
    row = lax.broadcasted_iota(jnp.int32, (SUB, tile), 0)
    upper, inverse, pending, corners = [], [], [], []
    for i in range(count):
        first = SUB * i
        own = blocks[i]
        corner = jnp.zeros((SUB, tile), jnp.float32)
        end = min(count, (i // group + 1) * group)
        if i % group == 0:
            ahead = [over_lanes(own, first + k, tile) for k in range(SUB)]
        cols, e = ahead, {}
        inside = (lane >= first) & (lane < first + SUB)
        later = {
            t: [over_lanes(blocks[t], first + k, tile) for k in range(SUB)]
            for t in range(i + 1, end)
        }
        if i + 1 < end:
            ahead = [over_lanes(blocks[i + 1], first + SUB + k, tile) for k in range(SUB)]
        rows = [
            jnp.where(inside, jnp.where(lane == first + j, 1.0, 0.0), over_rows(own, j, tile))
            for j in range(SUB)
        ]
        for j in range(SUB):
            line = [over_rows(cols[k], j, tile) for k in range(j, SUB)]
            s = lax.rsqrt(line[0])
            for k in range(j + 1, SUB):
                e[j, k] = line[k - j] * s
            down = cols[j] * s
            corner = jnp.where(lane == first + j, down, corner)
            for k in range(j + 1, SUB):
                cols[k] = cols[k] - down * e[j, k]
            rows[j] = rows[j] * s
            for t in later:
                later[t][j] = later[t][j] * s
            for k in range(j + 1, SUB):
                rows[k] = rows[k] - e[j, k] * rows[j]
                for t in later:
                    later[t][k] = later[t][k] - e[j, k] * later[t][j]
        if i + 1 < end:
            nxt = later[i + 1]
            for k in range(SUB):
                ahead[k] = ahead[k] - tree([nxt[j] * over_rows(nxt[j], k, tile) for j in range(SUB)])
        for t in later:
            update = tree([later[t][j] * rows[j] for j in range(SUB)])
            blocks[t] = jnp.where(inside, 0.0, blocks[t]) - update
        full = rows[0]
        for j in range(1, SUB):
            full = jnp.where(row == j, rows[j], full)
        corners.append(corner)
        pending.append(jnp.where((lane >= first + SUB) & (lane < SUB * end), 0.0, full))
        upper.append(jnp.where(lane >= first + SUB, full, 0.0))
        inverse.append(jnp.where(lane < first + SUB, full, 0.0))
        if i + 1 == end < count:
            done = jnp.concatenate(pending, 0)
            pending = []
            rest = SUB * end
            update = tn(done[:, rest:], done)
            here = (lane >= rest - group * SUB) & (lane < rest)
            for t in range(end, count):
                at = SUB * t - rest
                blocks[t] = jnp.where(here, 0.0, blocks[t]) - update[at:at + SUB, :]
        if i in hooks:
            hooks[i](inverse)
    across = lax.broadcasted_iota(jnp.int32, (tile, tile), 1)
    along = lax.broadcasted_iota(jnp.int32, (tile, tile), 0)
    corners = jnp.concatenate(corners, 0).T
    inner = (across >= along) & (across // SUB == along // SUB)
    upper = jnp.where(inner, corners, jnp.concatenate(upper, 0))
    return upper, jnp.concatenate(inverse, 0)


def back_kernel(points_total, chunks, part_ref, other_ref, *refs):
    sketch_refs = refs[:chunks]
    basis_out, factor_out, basis_ref, factor_ref, sem = refs[chunks:]
    tile = part_ref.shape[1]
    low = lax.axis_index("pts") % 2
    part = part_ref[...] / points_total
    other = other_ref[...] / points_total
    ends = jnp.where(low == 0, part[:tile], other[:tile])
    side = jnp.where(low == 0, other[:tile], part[:tile])
    diag = jnp.where(low == 0, other[tile:tile + 1], part[tile:tile + 1])
    row = lax.broadcasted_iota(jnp.int32, (tile, tile), 0)
    col = lax.broadcasted_iota(jnp.int32, (tile, tile), 1)
    ends_t = ends.T
    side_t = side.T
    split = lambda a: [a[SUB * t:SUB * (t + 1), :] for t in range(tile // SUB)]
    group = max(1, tile // SUB // 2)
    copies = []

    def put(src, dst):
        copies.append(pltpu.make_async_copy(src, dst, sem.at[len(copies)]))
        copies[-1].start()

    right = []
    rest = [jnp.where(row < col, ends, jnp.where(row == col, diag, ends_t))]

    def reduce_rest(inverse):
        inverse = jnp.concatenate(inverse[len(right) * group:(len(right) + 1) * group], 0)
        right.append(nn(inverse, side_t))
        rest.append(rest[-1] - nn(nt(side, inverse), right[-1]))

    last = tile // SUB - 1
    hooks = {min(last, end + 1): reduce_rest for end in range(group - 1, last, group)}
    hooks[last] = reduce_rest
    up, inv1 = panel(split(jnp.where(row >= col, ends, ends_t)), group, hooks)
    right = jnp.concatenate(right, 0)
    middle = []

    def first_half(_):
        factor_ref[:tile, :tile] = up
        factor_ref[tile:, :tile] = jnp.zeros((tile, tile), jnp.float32)
        factor_ref[:tile, tile:] = right
        sketch = jnp.concatenate([ref[...] for ref in sketch_refs], 0)
        left = nt(sketch[:, :tile], inv1)
        basis_ref[:, :tile] = left
        middle.append(sketch[:, tile:] - nn(left, right))
        put(factor_ref.at[:tile, :], factor_out.at[:tile, :])
        put(basis_ref.at[:, :tile], basis_out.at[:, :tile])

    up2, inv2 = panel(split(rest[-1]), group, {min(last, 1): first_half})
    middle = middle[0]
    basis_ref[:, tile:] = nt(middle, inv2)
    put(basis_ref.at[:, tile:], basis_out.at[:, tile:])
    factor_ref[tile:, tile:] = up2
    put(factor_ref.at[tile:, :], factor_out.at[tile:, :])
    for copy in copies:
        copy.wait()


def chunk_widths(own_rows):
    step = own_rows // 4
    if step % 128:
        return [own_rows]
    return [step] * 4


def on_device(precip, thresholds, bin_index, test_matrix):
    tm_count = lax.axis_size("tm")
    pts_count = lax.axis_size("pts")
    days_local, points_local = precip.shape
    columns = test_matrix.shape[1]
    tile = columns // 2
    own_rows = points_local // tm_count
    days_total = days_local * tm_count
    points_total = points_local * pts_count
    f32 = jnp.float32

    rows = harmonic_filter(days_total)
    filt = rows.reshape(rows.shape[0], tm_count, days_local).transpose(1, 0, 2)
    filt = jnp.asarray(filt)
    thr = thresholds[:, None]
    bins = bin_index[None, :]

    vmem = pl.BlockSpec(memory_space=pltpu.VMEM)
    widths = chunk_widths(own_rows)
    size = days_local // len(QUARTERS)
    mine = lax.dynamic_slice_in_dim(
        test_matrix, (lax.axis_index("pts") % len(QUARTERS)) * size, size, 0
    )
    shapes = [
        jax.ShapeDtypeStruct((days_local, width), f32)
        for width in widths
        for _ in range(tm_count - 1)
    ]
    pieces = pl.pallas_call(
        functools.partial(cut_kernel, widths, own_rows, tm_count),
        out_shape=shapes,
        in_specs=[pl.BlockSpec(memory_space=pl.ANY)],
        out_specs=[vmem] * len(shapes),
        scratch_shapes=[pltpu.SemaphoreType.DMA((len(shapes),))],
        compiler_params=pltpu.CompilerParams(vmem_limit_bytes=4 << 20),
        name="cut",
    )(precip)
    held = pl.pallas_call(
        hold_kernel,
        out_shape=jax.ShapeDtypeStruct(test_matrix.shape, f32),
        in_specs=[vmem],
        out_specs=vmem,
        compiler_params=pltpu.CompilerParams(vmem_limit_bytes=4 << 20),
        name="hold",
    )(test_matrix)
    sends = [("rows", mine, k) for k in range(1, tm_count)]
    for n in range(len(widths)):
        sends += [("points", pieces[n * (tm_count - 1) + k - 1], k) for k in range(1, tm_count)]
    came = []
    for _, value, k in sends:
        came.append(swap(value, k * pts_count))
    quarters, came = came[:tm_count - 1], came[tm_count - 1:]
    received = [came[n * (tm_count - 1):(n + 1) * (tm_count - 1)] for n in range(len(widths))]
    spread = []
    for got in quarters:
        beside = swap(got, 2)
        spread += [got, swap(got, 1)]
        spread += [beside, swap(beside, 1)]

    sketches, waiting = [], []
    cross = None
    start = 0
    for index, width in enumerate(widths):
        last = index == len(widths) - 1
        with_cross = last or sum(v.shape[0] for v in waiting) + width >= columns
        if sketches:
            received[index], sketches[-1] = lax.optimization_barrier((received[index], sketches[-1]))
        operands = [precip, thr, bins, filt, held] + received[index] + spread
        operands += waiting if with_cross else []
        operands += [cross] if with_cross and cross is not None else []
        shapes = [jax.ShapeDtypeStruct((width, columns), f32)]
        if last:
            shapes += [jax.ShapeDtypeStruct((tile + SUB, tile), f32)] * 2
        elif with_cross:
            shapes += [jax.ShapeDtypeStruct((columns, columns), f32)]
        out = pl.pallas_call(
            functools.partial(
                front_kernel,
                start,
                width,
                own_rows,
                tm_count,
                len(waiting) if with_cross else 0,
                with_cross and cross is not None,
                with_cross,
                last,
            ),
            out_shape=shapes,
            in_specs=[vmem] * len(operands),
            out_specs=[vmem] * len(shapes),
            scratch_shapes=[pltpu.VMEM((days_total, columns), f32)],
            cost_estimate=pl.CostEstimate(
                flops=12 * width * columns * (days_total + columns),
                bytes_accessed=4 * days_total * (width + columns),
                transcendentals=0,
            ),
            compiler_params=pltpu.CompilerParams(vmem_limit_bytes=16 << 20),
        )(*operands)
        sketches.append(out[0])
        if with_cross:
            waiting = []
            cross = out[1]
        else:
            waiting.append(out[0])
        start += width
    kept, sent = out[1], out[2]

    part = kept + swap(sent, 1)
    bits = [1 << n for n in range(1, (tm_count * pts_count).bit_length() - 1)]
    groups = []
    while bits:
        ends = {bits.pop(0), bits.pop() if bits else 0}
        groups.append(tuple(sorted(ends)) if len(ends) == 2 and 0 not in ends else (max(ends),))
    for even, odd in zip(groups, partners_order(groups)):
        steps = list(zip(partners(even), partners(odd)))
        got = [swap(part, *pair) for pair in steps]
        while len(got) > 1:
            got = [sum(got[n:n + 2][1:], got[n]) for n in range(0, len(got), 2)]
        part = part + got[0]
    other = swap(part, 1)

    basis, factor = pl.pallas_call(
        functools.partial(back_kernel, points_total, len(sketches)),
        out_shape=(
            jax.ShapeDtypeStruct((own_rows, columns), f32),
            jax.ShapeDtypeStruct((columns, columns), f32),
        ),
        in_specs=[vmem] * (2 + len(sketches)),
        out_specs=(pl.BlockSpec(memory_space=pltpu.HBM),) * 2,
        scratch_shapes=[
            pltpu.VMEM((own_rows, columns), f32),
            pltpu.VMEM((columns, columns), f32),
            pltpu.SemaphoreType.DMA((4,)),
        ],
        compiler_params=pltpu.CompilerParams(vmem_limit_bytes=16 << 20),
        name="back",
    )(part, other, *sketches)
    return basis, factor


def solution(mesh):
    in_specs = (P("tm", "pts"), P(), P("pts"), P("tm", None))
    out_specs = (P(("pts", "tm"), None), P())

    return jax.shard_map(
        on_device, mesh=mesh, in_specs=in_specs, out_specs=out_specs, check_vma=False
    )
```
